32 devices in a mesh: groups: 2 (over x), ctx: 8 (over z, y), head: 2 (over core).
Axes of the slice: x: 2, y: 2, z: 4, core: 2. Of those that a mesh axis runs over, the one named last changes fastest.
Arguments:
- x_in: bfloat16 [2048, 5120], P(('groups', 'ctx'), 'head'), parts along dimension 0, may hold values from -6 to 6
- bc_in: bfloat16 [2048, 256], P(('groups', 'ctx')), parts along dimension 0, may hold values from -1.5 to 1.5
- step_dt: float32 [2048, 80], P(('groups', 'ctx'), 'head'), parts along dimension 0, may hold values from 0.001 to 1.1, as said below
- a_log: float32 [80], P('head'), may hold values from -11.6 to 1.1
- d_skip: float32 [80], P('head'), may hold values from 0.5 to 2
- conv_wx: float32 [4, 5120], P(None, 'head'), may hold values from -3 to 3
- conv_bx: float32 [5120], P('head'), may hold values from -3 to 3
- conv_wbc: float32 [4, 256], replicated, may hold values from -3 to 3
- conv_bbc: float32 [256], replicated, may hold values from -0.12 to 0.12
- grad_out: bfloat16 [2048, 5120], P(('groups', 'ctx'), 'head'), parts along dimension 0, may hold values from -18 to 18
Outputs:
- y_out: bfloat16 [2048, 5120], P(('groups', 'ctx'), 'head'), parts along dimension 0
- grad_x_in: bfloat16 [2048, 5120], P(('groups', 'ctx'), 'head'), parts along dimension 0
- grad_bc_in: bfloat16 [2048, 256], P(('groups', 'ctx')), parts along dimension 0
- grad_step_dt: float32 [2048, 80], P(('groups', 'ctx'), 'head'), parts along dimension 0
- grad_a_log: float32 [160], P(('groups', 'head')), parts along dimension 0
- grad_d_skip: float32 [160], P(('groups', 'head')), parts along dimension 0
- grad_conv_wx: float32 [8, 5120], P('groups', 'head'), parts along dimension 0
- grad_conv_bx: float32 [10240], P(('groups', 'head')), parts along dimension 0
- grad_conv_wbc: float32 [8, 256], P('groups'), parts along dimension 0
- grad_conv_bbc: float32 [512], P('groups'), parts along dimension 0
The draws below stay inside these ranges and needn't reach their ends.
There are 2 independent parts, one for each index of `groups`. The reference program is written for one: setup_inputs(seed, part) draws one part's arguments, and reference() takes and returns one part's arrays. A program takes and returns all parts, laid end to end along the dimension named above; an argument that names none is the same for every part. Nothing has to cross between parts.
Inputs may be any that keep to these rules, and one draw needn't show every extreme that they name: `step_dt`: positive step sizes.
All inputs are finite; a program needn't handle non-finite values.
Results may differ from the reference program's by a relative error of at most 0.017.
Values may be sent and summed in bfloat16 or wider, within the bound.
No kernel may reach another device: no remote copies, remote signals or barrier semaphores. Data moves between devices by JAX's collectives and lax.ppermute only.
A program may use at most 192 MiB of HBM per device.

```python
import math
import jax
import jax.numpy as jnp
from jax import lax

HEAD_TOTAL = 80
HEAD_DIM = 64
STATE = 128
CONV = 4
BLOCK_LENGTH = 128
INNER = 5120
SEQUENCE_LENGTH = 1024
N_CTX = 8


def draw_step_dt(key, part):
    block_seed, jagged_seed, spike_seed, height_seed = jax.random.split(key, 4)
    segment_factor = jnp.exp(jax.random.uniform(block_seed, (N_CTX, HEAD_TOTAL), jnp.float32, math.log(0.5), math.log(2.0)))
    rough_samples = jax.random.uniform(jagged_seed, (SEQUENCE_LENGTH, HEAD_TOTAL), jnp.float32, 0.5, 1.5)
    baseline_steps = 0.05 * jnp.repeat(segment_factor, BLOCK_LENGTH, axis=0) * rough_samples
    spike_block = jax.random.randint(spike_seed, (), 0, N_CTX)
    position_index = jnp.arange(SEQUENCE_LENGTH, dtype=jnp.int32)
    spike_begin = spike_block * BLOCK_LENGTH + BLOCK_LENGTH // 4
    within_block = (position_index >= spike_begin) & (position_index < spike_begin + BLOCK_LENGTH // 2)
    spike_level = jax.random.uniform(height_seed, (SEQUENCE_LENGTH, HEAD_TOTAL), jnp.float32, 0.9, 1.1)
    return jnp.where(within_block[:, None], spike_level, baseline_steps)


def draw_a_log(key, part):
    base_seed, fast_seed, order_seed = jax.random.split(key, 3)
    base_rates = jax.random.uniform(base_seed, (HEAD_TOTAL,), jnp.float32, math.log(1e-05), math.log(0.5))
    fast_rates = jax.random.uniform(fast_seed, (HEAD_TOTAL,), jnp.float32, math.log(1.5), math.log(3.0))
    ranking = jax.random.permutation(order_seed, HEAD_TOTAL)
    return jnp.where(ranking < max(1, HEAD_TOTAL // 8), fast_rates, base_rates)


def draw_grad_out(key, part):
    ramp = jnp.arange(SEQUENCE_LENGTH, dtype=jnp.float32) / SEQUENCE_LENGTH
    values = jax.random.normal(key, (SEQUENCE_LENGTH, INNER), jnp.float32)
    values = jnp.clip(values, -6.0, 6.0) * (1.0 + 2.0 * ramp)[:, None]
    return values.astype(jnp.bfloat16)


def block_scale(stream_key, extent, shards, least, high):
    level = 1.0
    for dim, shards_of in shards:
        heights = jax.random.uniform(jax.random.fold_in(jax.random.fold_in(stream_key, 6), dim), (shards_of,), jnp.float32, least / len(shards), high / len(shards))
        level = level * jnp.repeat(jnp.exp(heights), extent[dim] // shards_of).reshape((-1,) + (1,) * (len(extent) - 1 - dim))
    return level


def bell_draw(key, dims, width, most, cuts=(), held_as=jnp.bfloat16):
    gain = block_scale(key, dims, cuts, -0.22, 0.18) if cuts else 1.0
    result = jax.random.normal(key, dims, jnp.float32) * width * gain
    return jnp.minimum(jnp.maximum(result, -most), most).astype(held_as)


def setup_inputs(seed: int = 0, part: int = 0) -> dict:
    seeds = jax.random.split(jax.random.key(seed), 11)
    part_splits = jax.random.split(jax.random.fold_in(seeds[10], part), 11)
    return {
        "x_in": bell_draw(part_splits[0], (SEQUENCE_LENGTH, INNER), 1.0, 6.0, ((0, 8), (1, 2))),
        "bc_in": bell_draw(part_splits[1], (SEQUENCE_LENGTH, 2 * STATE), 0.25, 1.5, ((0, 8),)),
        "step_dt": draw_step_dt(jax.random.fold_in(jax.random.fold_in(seeds[10], part), 71), part),
        "a_log": draw_a_log(jax.random.fold_in(seeds[10], 71), part),
        "d_skip": jnp.clip(0.5 + 1.5 * jax.random.uniform(seeds[4], (HEAD_TOTAL,), jnp.float32) ** block_scale(seeds[4], (HEAD_TOTAL,), ((0, 2),), -0.2, 0.2), 0.5, 2.0),
        "conv_wx": bell_draw(seeds[5], (CONV, INNER), CONV ** -0.5, 3.0, ((1, 2),), jnp.float32),
        "conv_bx": bell_draw(seeds[6], (INNER,), 0.5, 3.0, ((0, 2),), jnp.float32),
        "conv_wbc": bell_draw(seeds[7], (CONV, 2 * STATE), CONV ** -0.5, 3.0, (), jnp.float32),
        "conv_bbc": bell_draw(seeds[8], (2 * STATE,), 0.02, 0.12, (), jnp.float32),
        "grad_out": draw_grad_out(jax.random.fold_in(jax.random.fold_in(seeds[10], part), 71), part),
    }


def conv_silu(padded, weight, bias):
    row_count = padded.shape[0] - weight.shape[0] + 1
    summed = bias[None, :]
    for tap_index in range(weight.shape[0]):
        summed = summed + weight[tap_index][None, :] * padded[tap_index:tap_index + row_count]
    return jax.nn.silu(summed).astype(jnp.bfloat16)

def section_one(x_pad, bc_pad, step_dt, a_log, d_skip, conv_wx, conv_bx, conv_wbc, conv_bbc):
    mixed_x = conv_silu(x_pad, conv_wx, conv_bx)
    mixed_bc = conv_silu(bc_pad, conv_wbc, conv_bbc)
    state_count = mixed_bc.shape[1] // 2
    b_matrix = mixed_bc[:, :state_count]
    c_matrix = mixed_bc[:, state_count:]
    row_count, head_count = step_dt.shape
    head_width = mixed_x.shape[1] // head_count
    decay_rate = -step_dt * jnp.exp(a_log)[None, :]
    cumulative = jnp.cumsum(decay_rate, axis=0)
    totals = jnp.exp(cumulative[-1])
    scores = jnp.dot(c_matrix, b_matrix.T, preferred_element_type=jnp.float32)
    causal = jnp.arange(row_count)[:, None] >= jnp.arange(row_count)[None, :]
    spread_gap = cumulative.T[:, :, None] - cumulative.T[:, None, :]
    decays = jnp.where(causal[None], jnp.exp(jnp.where(causal[None], spread_gap, 0.0)), 0.0)
    mixing = (decays * scores[None] * step_dt.T[:, None, :]).astype(jnp.bfloat16)
    heads_x = mixed_x.reshape(row_count, head_count, head_width)
    intra_part = jnp.einsum('htr,rhp->thp', mixing.astype(jnp.float32), heads_x.astype(jnp.float32))
    end_weight = jnp.exp(cumulative[-1][None, :] - cumulative) * step_dt
    weighted = (heads_x.astype(jnp.float32) * end_weight[:, :, None]).astype(jnp.bfloat16)
    block_state = jnp.einsum('rhp,rn->hpn', weighted.astype(jnp.float32), b_matrix.astype(jnp.float32))
    local_out = intra_part + d_skip[None, :, None] * heads_x.astype(jnp.float32)
    return (totals, block_state, local_out.reshape(row_count, head_count * head_width), c_matrix, cumulative)

def section_two(local_out, c_matrix, cumulative, carried):
    row_count = cumulative.shape[0]
    inter_part = jnp.einsum('tn,hpn->thp', c_matrix.astype(jnp.float32), carried, precision=lax.Precision.HIGHEST)
    inter_part = inter_part * jnp.exp(cumulative)[:, :, None]
    return local_out + inter_part.reshape(row_count, -1)

def reference(x_in, bc_in, step_dt, a_log, d_skip, conv_wx, conv_bx, conv_wbc, conv_bbc, grad_out):
    margin = CONV - 1

    def forward(x_wide, bc_wide, step_dt, a_log, d_skip, conv_wx, conv_bx, conv_wbc, conv_bbc):
        x_pad = jnp.concatenate([jnp.zeros((margin, x_wide.shape[1]), jnp.float32), x_wide])
        bc_pad = jnp.concatenate([jnp.zeros((margin, bc_wide.shape[1]), jnp.float32), bc_wide])

        def block_step(carried, position):
            offset = (position * BLOCK_LENGTH).astype(jnp.int32)
            totals, block_state, local_out, c_matrix, cumulative = section_one(lax.dynamic_slice_in_dim(x_pad, offset, BLOCK_LENGTH + margin, 0), lax.dynamic_slice_in_dim(bc_pad, offset, BLOCK_LENGTH + margin, 0), lax.dynamic_slice_in_dim(step_dt, offset, BLOCK_LENGTH, 0), a_log, d_skip, conv_wx, conv_bx, conv_wbc, conv_bbc)
            outputs = section_two(local_out, c_matrix, cumulative, carried)
            return (totals[:, None, None] * carried + block_state, outputs)
        initial = jnp.zeros((HEAD_TOTAL, HEAD_DIM, STATE), jnp.float32)
        final_state, outputs = lax.scan(jax.checkpoint(block_step), initial, jnp.arange(N_CTX, dtype=jnp.int32))
        return outputs.reshape(SEQUENCE_LENGTH, HEAD_TOTAL * HEAD_DIM)
    y_full, backward = jax.vjp(forward, x_in.astype(jnp.float32), bc_in.astype(jnp.float32), step_dt, a_log, d_skip, conv_wx, conv_bx, conv_wbc, conv_bbc)
    gradients = backward(grad_out.astype(jnp.float32))
    return (y_full.astype(jnp.bfloat16), gradients[0].astype(jnp.bfloat16), gradients[1].astype(jnp.bfloat16), gradients[2], gradients[3], gradients[4], gradients[5], gradients[6], gradients[7], gradients[8])
```

```python
import functools

import jax
import jax.numpy as jnp
from jax import lax
from jax.experimental import pallas as pl
from jax.experimental.pallas import tpu as pltpu
from jax.sharding import PartitionSpec as P

F32, BF16 = jnp.float32, jnp.bfloat16
EXACT = lax.Precision.HIGHEST
LANES = 128
HALO = 8


def dot(a, b, ca=1, cb=0, precision=None):
    dims = (((ca,), (cb,)), ((), ()))
    return lax.dot_general(a, b, dims, preferred_element_type=F32, precision=precision)


def iota(shape, dim):
    return lax.broadcasted_iota(jnp.int32, shape, dim)


def lower_ones(size):
    return (iota((size, size), 0) >= iota((size, size), 1)).astype(F32)


def upper_ones(size):
    return (iota((size, size), 0) <= iota((size, size), 1)).astype(F32)


def sigmoid(v):
    return 1.0 / (1.0 + jnp.exp(-v))


def cols(start):
    return pl.ds(pl.multiple_of(start, LANES), LANES)


class Sizes:
    def __init__(self, rows, width, heads, state, group):
        self.rows, self.width, self.heads, self.state, self.group = rows, width, heads, state, group
        self.head_dim = width // heads
        self.lane_width = width // group
        self.lane_heads = heads // group
        self.chunks = self.lane_width // LANES
        self.per_chunk = LANES // self.head_dim


def lane_slices(s, value, scratch):
    for lane in range(s.group):
        scratch[lane, :, 0 : s.lane_heads] = value[:, lane * s.lane_heads : (lane + 1) * s.lane_heads]


def lane_join(s, scratch):
    return jnp.concatenate([scratch[lane][:, 0 : s.lane_heads] for lane in range(s.group)], axis=1)


def spread(s, value, chunk):
    rows = value.shape[0]
    lane = iota((rows, LANES), 1)
    out = None
    for i in range(s.per_chunk):
        h = chunk * s.per_chunk + i
        col = jnp.broadcast_to(value[:, h : h + 1], (rows, LANES))
        out = col if out is None else jnp.where(lane >= i * s.head_dim, col, out)
    return out


def head_sum_matrix(s, chunk):
    r, c = iota((LANES, LANES), 0), iota((LANES, LANES), 1)
    one = (c == chunk * s.per_chunk + r // s.head_dim).astype(F32).astype(BF16)
    return jnp.concatenate([one, one], axis=0)


def head_sums(s, value, chunk):
    hi = value.astype(BF16)
    lo = (value - hi.astype(F32)).astype(BF16)
    return dot(jnp.concatenate([hi, lo], axis=1), head_sum_matrix(s, chunk))


def decay(step, alog):
    rate = -step * jnp.exp(alog)
    return rate, dot(lower_ones(step.shape[0]), rate, precision=EXACT)


def conv_into(buf, halo, x, weight, bias):
    rows = x.shape[0]
    buf[0:HALO, :] = halo.astype(F32)
    buf[HALO : HALO + rows, :] = x.astype(F32)
    taps = weight.shape[0]
    total = jnp.broadcast_to(bias, x.shape)
    for k in range(taps):
        first = HALO - (taps - 1) + k
        total = total + weight[k : k + 1, :] * buf[first : first + rows, :]
    return total


def states_kernel(s, lane_ref, x_ref, halo_ref, bc_ref, g_ref, dt_ref, al_ref, wx_ref, bx_ref, wbc_ref, bbc_ref, mx_ref, mbc_ref, *rest):
    outs = rest[: s.group]
    msg, endw_s, ecum_s, wx_s, ge_s, xbuf, bbuf, sems = rest[s.group :]
    me = lane_ref[0]
    _, cum = decay(dt_ref[...], al_ref[...])
    last = cum[s.rows - 1 : s.rows, :]
    lane_slices(s, jnp.exp(last - cum) * dt_ref[...], endw_s)
    lane_slices(s, jnp.exp(cum), ecum_s)
    total8 = jnp.broadcast_to(jnp.exp(last), (8, s.heads))
    v = conv_into(bbuf, halo_ref[:, s.width :], bc_ref[...], wbc_ref[...], bbc_ref[...])
    mixed_bc = v * sigmoid(v)
    mbc_ref[...] = mixed_bc.astype(BF16)
    mixed_bc = mixed_bc.astype(BF16).astype(F32)
    b_t = jnp.transpose(mixed_bc[:, : s.state]).astype(BF16)
    c_t = jnp.transpose(mixed_bc[:, s.state :]).astype(BF16)

    def lane_body(lane, carry):
        base = lane * s.lane_width
        for c in range(s.chunks):
            at = cols(base + c * LANES)
            here = slice(c * LANES, (c + 1) * LANES)
            v = conv_into(xbuf.at[c], halo_ref[:, at], x_ref[:, at], wx_ref[:, at], bx_ref[:, at])
            mixed = (v * sigmoid(v)).astype(BF16)
            mx_ref[:, at] = mixed
            wx_s[:, here] = (mixed.astype(F32) * spread(s, endw_s[lane], c)).astype(BF16)
            ge_s[:, here] = (g_ref[:, at].astype(F32) * spread(s, ecum_s[lane], c)).astype(BF16)
        rows = slice(0, s.state)
        msg[lane, rows, : s.lane_width] = dot(b_t, wx_s[...]).astype(BF16)
        msg[lane, rows, s.lane_width :] = dot(c_t, ge_s[...]).astype(BF16)
        shape = (s.heads, s.lane_width)
        pick = (iota(shape, 0) == lane * s.lane_heads + iota(shape, 1) // s.head_dim).astype(F32)
        total = dot(total8, pick, precision=EXACT)
        hi = total.astype(BF16).astype(F32)
        mid = (total - hi).astype(BF16).astype(F32)
        low = total - hi - mid
        row = iota(total.shape, 0)
        parts = jnp.where(row == 0, hi, jnp.where(row == 1, mid, jnp.where(row == 2, low, 0.0)))
        msg[lane, s.state : s.state + 8, : s.lane_width] = parts.astype(BF16)
        msg[lane, s.state : s.state + 8, s.lane_width :] = parts.astype(BF16)
        return carry

    lax.fori_loop(0, s.group, lane_body, 0)
    copies = [pltpu.make_async_copy(msg.at[me ^ d], outs[d], sems.at[d]) for d in range(s.group)]
    for c in copies:
        c.start()
    for c in copies:
        c.wait()


def intra_kernel(s, mx_ref, g_ref, mbc_ref, dt_ref, dtt_ref, al_ref, alt_ref, dsk_ref, y_ref, dx_ref, rs_ref, vs_ref, dbc_ref, cum_s, cumt_s, dtt_s, rs_s, vs_s):
    rows = s.rows
    _, cum = decay(dt_ref[...], al_ref[...])
    lane_slices(s, cum, cum_s)
    step_t = dtt_ref[...]
    cum_t = dot(-step_t * jnp.exp(alt_ref[...]), upper_ones(rows), precision=EXACT)
    for lane in range(s.group):
        heads = slice(lane * s.lane_heads, (lane + 1) * s.lane_heads)
        cumt_s[lane, 0 : s.lane_heads, :] = cum_t[heads, :]
        dtt_s[lane, 0 : s.lane_heads, :] = step_t[heads, :]
    b, c_m = mbc_ref[:, : s.state], mbc_ref[:, s.state :]
    causal = iota((rows, rows), 0) >= iota((rows, rows), 1)
    scores = jnp.where(causal, dot(c_m, b, 1, 1), 0.0)
    lane_id = iota((rows, LANES), 1)
    masks = [((lane_id >= i * s.head_dim) & (lane_id < (i + 1) * s.head_dim)).astype(F32).astype(BF16) for i in range(s.per_chunk)]

    def lane_body(lane, d_scores):
        base = lane * s.lane_width
        row_acc = jnp.zeros((rows, LANES), F32)
        col_acc = jnp.zeros((rows, LANES), F32)
        cum_l = cum_s[lane]
        for c in range(s.chunks):
            at = cols(base + c * LANES)
            x, g = mx_ref[:, at], g_ref[:, at]
            x_st = jnp.concatenate([x * m for m in masks], axis=0)
            g_st = jnp.concatenate([g * m for m in masks], axis=0)
            d_mix = dot(g_st, x, 1, 1)
            mixes = []
            for i in range(s.per_chunk):
                h = c * s.per_chunk + i
                gap = jnp.broadcast_to(cum_l[:, h : h + 1], (rows, rows)) - cumt_s[lane, h : h + 1, :]
                e = jnp.exp(jnp.minimum(gap, 0.0)) * dtt_s[lane, h : h + 1, :]
                mixes.append((e * scores).astype(BF16))
                d_scores = d_scores + d_mix[i * rows : (i + 1) * rows, :] * e
            y = dot(jnp.concatenate(mixes, axis=1), x_st)
            dx = dot(jnp.concatenate(mixes, axis=0), g_st, 0, 0)
            xf, gf, skip = x.astype(F32), g.astype(F32), dsk_ref[:, at]
            row_acc = row_acc + head_sums(s, gf * y, c)
            col_acc = col_acc + head_sums(s, xf * dx, c)
            y_ref[:, at] = (y + skip * xf).astype(BF16)
            dx_ref[:, at] = (dx + skip * gf).astype(BF16)
        rs_s[lane] = row_acc
        vs_s[lane] = col_acc
        return d_scores

    d_scores = lax.fori_loop(0, s.group, lane_body, jnp.zeros((rows, rows), F32))
    d_scores = jnp.where(causal, d_scores, 0.0).astype(BF16)
    rs_ref[...] = lane_join(s, rs_s)
    vs_ref[...] = lane_join(s, vs_s)
    dbc_ref[:, : s.state] = dot(d_scores, c_m, 0, 0)
    dbc_ref[:, s.state :] = dot(d_scores, b)


def gather_blocks(s, me, srcs, buf, sems):
    copies = [pltpu.make_async_copy(srcs[d], buf.at[me ^ d], sems.at[d]) for d in range(s.group)]
    for c in copies:
        c.start()
    for c in copies:
        c.wait()


def total_row(s, buf, i, at):
    return jnp.sum(buf[i, s.state : s.state + 8, at].astype(F32), axis=0, keepdims=True)


def group_sum_kernel(s, pair, at_ref, *refs):
    srcs, (buf, sems) = refs[: s.group], refs[-2:]
    outs = refs[s.group : -2]
    me, high = at_ref[0], at_ref[1]
    gather_blocks(s, me, srcs, buf, sems)
    for c in range(s.chunks):
        at = slice(c * LANES, (c + 1) * LANES)
        at_r = slice(s.lane_width + c * LANES, s.lane_width + (c + 1) * LANES)
        totals = [total_row(s, buf, i, at) for i in range(s.group)]
        ahead = jnp.zeros((s.state, LANES), F32)
        back = jnp.zeros((s.state, LANES), F32)
        every = jnp.ones((1, LANES), F32)
        for i in range(s.group):
            ahead = totals[i] * ahead + buf[i, 0 : s.state, at].astype(F32)
            r = s.group - 1 - i
            back = totals[r] * back + buf[r, 0 : s.state, at_r].astype(F32)
            every = every * totals[i]
        if pair:
            outs[0][:, at] = jnp.where(high == 0, ahead, back).astype(BF16)
        else:
            outs[0][:, at] = ahead.astype(BF16)
            outs[1][:, at] = back.astype(BF16)
            outs[2][:, at] = jnp.broadcast_to(every, (8, LANES))


def group_scan_kernel(s, pair, at_ref, *refs):
    srcs = refs[: s.group]
    n_in = 1 if pair else 2
    before = refs[s.group : s.group + n_in]
    outs = refs[s.group + n_in : 2 * s.group + n_in]
    buf, done, sems, out_sems = refs[2 * s.group + n_in :]
    me, high = at_ref[0], at_ref[1]
    gather_blocks(s, me, srcs, buf, sems)
    for c in range(s.chunks):
        at = slice(c * LANES, (c + 1) * LANES)
        at_r = slice(s.lane_width + c * LANES, s.lane_width + (c + 1) * LANES)
        totals = [total_row(s, buf, i, at) for i in range(s.group)]
        first = before[0][:, at].astype(F32)
        if pair:
            ahead = jnp.where(high == 1, first, 0.0)
            back = jnp.where(high == 0, first, 0.0)
        else:
            ahead, back = first, before[1][:, at].astype(F32)
        for i in range(s.group):
            done[i, :, at] = ahead.astype(BF16)
            r = s.group - 1 - i
            done[r, :, at_r] = back.astype(BF16)
            if i < s.group - 1:
                ahead = totals[i] * ahead + buf[i, 0 : s.state, at].astype(F32)
                back = totals[r] * back + buf[r, 0 : s.state, at_r].astype(F32)
    copies = [pltpu.make_async_copy(done.at[me ^ d], outs[d], out_sems.at[d]) for d in range(s.group)]
    for c in copies:
        c.start()
    for c in copies:
        c.wait()


def conv_back(buf, dv, weight):
    rows, taps = dv.shape[0], weight.shape[0]
    zeros = jnp.zeros((HALO, dv.shape[1]), F32)
    buf[0:HALO, :] = zeros
    buf[HALO : HALO + rows, :] = dv
    buf[HALO + rows : 2 * HALO + rows, :] = zeros
    own = before = None
    for k in range(taps):
        w = weight[k : k + 1, :]
        first = HALO + taps - 1 - k
        part = w * buf[first : first + rows, :]
        own = part if own is None else own + part
        first = taps - 1 - k
        part = w * buf[first : first + HALO, :]
        before = part if before is None else before + part
    keep = iota(before.shape, 0) >= HALO - (taps - 1)
    return own, jnp.where(keep, before, 0.0)


def conv_weight_rows(buf, dv, taps):
    rows = dv.shape[0]
    out = []
    for k in range(taps):
        first = HALO - (taps - 1) + k
        out.append(jnp.sum(dv * buf[first : first + rows, :], axis=0, keepdims=True))
    out.append(jnp.sum(dv, axis=0, keepdims=True))
    return out


def silu_slope(v):
    sig = sigmoid(v)
    return sig * (1.0 + v * (1.0 - sig))


def final_kernel(s, lane_ref, x_ref, halo_ref, bc_ref, g_ref, dt_ref, al_ref, wx_ref, bx_ref, wbc_ref, bbc_ref, mx_ref, mbc_ref, yl_ref, dxl_ref, rs_ref, vs_ref, dbc_ref, *rest):
    srcs = rest[: s.group]
    y_ref, gx_ref, ho_ref, gdt_ref, gal_ref, pk_ref, gbc_ref = rest[s.group : s.group + 7]
    held, endw_s, ecum_s, wx_s, ge_s, xbuf, dbuf, bbuf, dbbuf, rs_s, us_s, hl_s, sems = rest[s.group + 7 :]
    me = lane_ref[0]
    copies = [pltpu.make_async_copy(srcs[d], held.at[me ^ d], sems.at[d]) for d in range(s.group)]
    for c in copies:
        c.start()
    rows, taps = s.rows, wx_ref.shape[0]
    rate, cum = decay(dt_ref[...], al_ref[...])
    last = cum[rows - 1 : rows, :]
    lane_slices(s, jnp.exp(last - cum) * dt_ref[...], endw_s)
    lane_slices(s, jnp.exp(cum), ecum_s)
    b, c_m = mbc_ref[:, : s.state], mbc_ref[:, s.state :]
    shape = (s.lane_width, LANES)
    pick = (iota(shape, 0) // s.head_dim == iota(shape, 1)).astype(F32)
    for c in copies:
        c.wait()

    def lane_body(lane, carry):
        d_b, d_c = carry
        base = lane * s.lane_width
        row_acc = jnp.zeros((rows, LANES), F32)
        col_acc = jnp.zeros((rows, LANES), F32)
        links = []
        for c in range(s.chunks):
            at = cols(base + c * LANES)
            here = slice(c * LANES, (c + 1) * LANES)
            here_r = slice(s.lane_width + c * LANES, s.lane_width + (c + 1) * LANES)
            state, later = held[lane, :, here], held[lane, :, here_r]
            xf, gf = mx_ref[:, at].astype(F32), g_ref[:, at].astype(F32)
            grow = spread(s, ecum_s[lane], c)
            shrink = spread(s, endw_s[lane], c)
            y = dot(c_m, state) * grow
            y_ref[:, at] = (yl_ref[:, at].astype(F32) + y).astype(BF16)
            row_acc = row_acc + head_sums(s, gf * y, c)
            dx = dot(b, later) * shrink
            col_acc = col_acc + head_sums(s, xf * dx, c)
            ge_s[:, here] = (gf * grow).astype(BF16)
            wx_s[:, here] = (xf * shrink).astype(BF16)
            links.append(jnp.sum(state.astype(F32) * later.astype(F32), axis=0, keepdims=True))
            weight = wx_ref[:, at]
            v = conv_into(xbuf.at[c], halo_ref[:, at], x_ref[:, at], weight, bx_ref[:, at])
            dv = (dxl_ref[:, at].astype(F32) + dx) * silu_slope(v)
            own, before = conv_back(dbuf.at[c], dv, weight)
            gx_ref[:, at] = own.astype(BF16)
            ho_ref[:, at] = before.astype(BF16)
            packed = conv_weight_rows(xbuf.at[c], dv, taps)
            packed.append(jnp.sum(gf * xf, axis=0, keepdims=True))
            packed.append(jnp.zeros((8 - len(packed), LANES), F32))
            pk_ref[:, at] = jnp.concatenate(packed, axis=0)
        rs_s[lane] = row_acc
        us_s[lane] = col_acc
        link = jnp.broadcast_to(jnp.concatenate(links, axis=1), (8, s.lane_width))
        hl_s[lane] = dot(link, pick, precision=EXACT)
        d_c = d_c + dot(ge_s[...], held[lane, :, : s.lane_width], 1, 1)
        d_b = d_b + dot(wx_s[...], held[lane, :, s.lane_width :], 1, 1)
        return d_b, d_c

    zero = jnp.zeros((rows, s.state), F32)
    d_b, d_c = lax.fori_loop(0, s.group, lane_body, (zero, zero))
    inter = lane_join(s, us_s)
    through = vs_ref[...] + inter
    d_cum = rs_ref[...] + lane_join(s, rs_s) - through
    d_last = jnp.sum(inter, axis=0, keepdims=True) + jnp.exp(last) * lane_join(s, hl_s)[0:1, :]
    d_cum = d_cum + jnp.where(iota(d_cum.shape, 0) == rows - 1, d_last, 0.0)
    d_rate = dot(upper_ones(rows), d_cum, precision=EXACT)
    step = dt_ref[...]
    gdt_ref[...] = through / step - jnp.exp(al_ref[...]) * d_rate
    gal_ref[...] = jnp.sum(rate * d_rate, axis=0, keepdims=True)

    v = conv_into(bbuf, halo_ref[:, s.width :], bc_ref[...], wbc_ref[...], bbc_ref[...])
    dv = (dbc_ref[...] + jnp.concatenate([d_b, d_c], axis=1)) * silu_slope(v)
    own, before = conv_back(dbbuf, dv, wbc_ref[...])
    gbc_ref[0:rows, :] = own.astype(BF16)
    gbc_ref[rows : rows + HALO, :] = before.astype(BF16)
    packed = conv_weight_rows(bbuf, dv, taps)
    packed.append(jnp.zeros((8 - len(packed), 2 * s.state), F32))
    gbc_ref[rows + HALO : rows + 2 * HALO, :] = jnp.concatenate(packed, axis=0).astype(BF16)


VMEM = pl.BlockSpec(memory_space=pltpu.VMEM)
SMEM = pl.BlockSpec(memory_space=pltpu.SMEM)
ANY = pl.BlockSpec(memory_space=pl.ANY)


def call(kernel, name, args, in_specs, outs, out_specs, scratch, flops, limit=48):
    moved = sum(a.size * a.dtype.itemsize for a in (*args, *outs))
    return pl.pallas_call(
        kernel,
        name=name,
        out_shape=tuple(outs),
        in_specs=in_specs,
        out_specs=tuple(out_specs),
        scratch_shapes=scratch,
        compiler_params=pltpu.CompilerParams(vmem_limit_bytes=limit << 20),
        cost_estimate=pl.CostEstimate(flops=flops, bytes_accessed=moved, transcendentals=0),
    )(*args)


def shift(value, count, steps):
    pairs = [(i, i + steps) for i in range(count) if 0 <= i + steps < count]
    return lax.ppermute(value, "ctx", pairs)


def swap(value, count, mask):
    return lax.ppermute(value, "ctx", [(i, i ^ mask) for i in range(count)])


def ctx_sum(value, count):
    step = 1
    while step < count:
        value = value + swap(value, count, step)
        step *= 2
    return value


def group_scan(ahead, back, every, count, group):
    found = []
    for sign, value in ((1, ahead), (-1, back)):
        total = shift(every, count, sign * group)
        value = shift(value, count, sign * group).astype(F32)
        step = group
        while step < count:
            value = value + total[0:1] * shift(value.astype(BF16), count, sign * step).astype(F32)
            total = total * shift(total, count, sign * step)
            step *= 2
        found.append(value.astype(BF16))
    return found


def local(n_ctx, x_in, bc_in, step_dt, a_log, d_skip, conv_wx, conv_bx, conv_wbc, conv_bbc, grad_out):
    rows, width = x_in.shape
    heads, state = step_dt.shape[1], bc_in.shape[1] // 2
    group = 4
    s = Sizes(rows, width, heads, state, group)
    n_group = n_ctx // group
    pair = n_group == 2
    index = lax.axis_index("ctx")
    place = jnp.stack([index % group, index // group]).astype(jnp.int32)
    sds = jax.ShapeDtypeStruct
    lw = s.lane_width

    halo = shift(jnp.concatenate([x_in[-HALO:], bc_in[-HALO:]], axis=1), n_ctx, 1)
    al, bx, bbc = a_log[None, :], conv_bx[None, :], conv_bbc[None, :]
    msg_rows = state + 8
    matmul = 2 * rows * width * state
    per_head = pltpu.VMEM((group, rows, LANES), F32)
    sems = pltpu.SemaphoreType.DMA((group,))
    conv_args = (x_in, halo, bc_in, grad_out, step_dt, al, conv_wx, bx, conv_wbc, bbc)
    mx, mbc, *msgs = call(
        functools.partial(states_kernel, s),
        "states",
        (place, *conv_args),
        [SMEM] + [VMEM] * len(conv_args),
        [sds((rows, width), BF16), sds((rows, 2 * state), BF16)] + [sds((msg_rows, 2 * lw), BF16)] * group,
        [VMEM, VMEM] + [ANY] * group,
        [
            pltpu.VMEM((group, msg_rows, 2 * lw), BF16),
            per_head,
            per_head,
            pltpu.VMEM((rows, lw), BF16),
            pltpu.VMEM((rows, lw), BF16),
            pltpu.VMEM((s.chunks, rows + HALO, LANES), F32),
            pltpu.VMEM((rows + HALO, 2 * state), F32),
            sems,
        ],
        2 * matmul,
    )
    blocks = [msgs[0]] + [swap(msgs[d], n_ctx, d) for d in range(1, group)]

    intra_args = (mx, grad_out, mbc, step_dt, step_dt.T, al, a_log[:, None], jnp.repeat(d_skip, s.head_dim)[None, :])
    per_row = pltpu.VMEM((group, 16, rows), F32)
    yl, dxl, rs, vs, dbc = call(
        functools.partial(intra_kernel, s),
        "intra",
        intra_args,
        [VMEM] * len(intra_args),
        [sds((rows, width), BF16)] * 2 + [sds((rows, heads), F32)] * 2 + [sds((rows, 2 * state), F32)],
        [VMEM] * 5,
        [per_head, per_row, per_row, per_head, per_head],
        6 * matmul,
    )

    buf = pltpu.VMEM((group, msg_rows, 2 * lw), BF16)
    if pair:
        sums = [sds((state, lw), BF16)]
    else:
        sums = [sds((state, lw), BF16)] * 2 + [sds((8, lw), F32)]
    summed = call(
        functools.partial(group_sum_kernel, s, pair),
        "group_sum",
        (place, *blocks),
        [SMEM] + [ANY] * group,
        sums,
        [VMEM] * len(sums),
        [buf, sems],
        state * width,
    )
    if pair:
        before = [swap(summed[0], n_ctx, group)]
    else:
        before = group_scan(*summed, n_ctx, group)
    sends = call(
        functools.partial(group_scan_kernel, s, pair),
        "group_scan",
        (place, *blocks, *before),
        [SMEM] + [ANY] * group + [VMEM] * len(before),
        [sds((state, 2 * lw), BF16)] * group,
        [ANY] * group,
        [buf, pltpu.VMEM((group, state, 2 * lw), BF16), sems, sems],
        state * width,
    )
    held = [sends[0]] + [swap(sends[d], n_ctx, d) for d in range(1, group)]

    final_args = (*conv_args, mx, mbc, yl, dxl, rs, vs, dbc)
    y, gx, before_x, gdt, gal, packed, gbc = call(
        functools.partial(final_kernel, s),
        "final",
        (place, *final_args, *held),
        [SMEM] + [VMEM] * len(final_args) + [ANY] * group,
        [
            sds((rows, width), BF16),
            sds((rows, width), BF16),
            sds((HALO, width), BF16),
            sds((rows, heads), F32),
            sds((1, heads), F32),
            sds((8, width), F32),
            sds((rows + 2 * HALO, 2 * state), BF16),
        ],
        [VMEM] * 7,
        [
            pltpu.VMEM((group, state, 2 * lw), BF16),
            per_head,
            per_head,
            pltpu.VMEM((rows, lw), BF16),
            pltpu.VMEM((rows, lw), BF16),
            pltpu.VMEM((s.chunks, rows + HALO, LANES), F32),
            pltpu.VMEM((s.chunks, rows + 2 * HALO, LANES), F32),
            pltpu.VMEM((rows + HALO, 2 * state), F32),
            pltpu.VMEM((rows + 2 * HALO, 2 * state), F32),
            per_head,
            per_head,
            pltpu.VMEM((group, 8, LANES), F32),
            sems,
        ],
        4 * matmul,
    )

    n_head = lax.axis_size("head")
    gbc = gbc.astype(F32)
    step = 1
    while step < n_head:
        other = lax.ppermute(gbc.astype(BF16), "head", [(i, i ^ step) for i in range(n_head)])
        gbc = gbc + other.astype(F32)
        step *= 2
    back = jnp.concatenate([before_x, gbc[rows : rows + HALO].astype(BF16)], axis=1)
    back = shift(back, n_ctx, -1)
    tail = gx[-HALO:].astype(F32) + back[:, :width].astype(F32)
    gx = lax.dynamic_update_slice(gx, tail.astype(BF16), (rows - HALO, 0))
    tail = gbc[rows - HALO : rows] + back[:, width:].astype(F32)
    grad_bc = jnp.concatenate([gbc[: rows - HALO], tail]).astype(BF16)

    taps = conv_wx.shape[0]
    bc_sums = gbc[rows + HALO : rows + HALO + taps + 1].reshape(-1)
    small = jnp.concatenate([gal[0], bc_sums])
    small = jnp.pad(small, (0, width - small.shape[0]))
    packed = jnp.concatenate([packed[: taps + 2], small[None, :], jnp.zeros((1, width), F32)])
    packed = ctx_sum(packed, n_ctx)
    grad_skip = packed[taps + 1].reshape(heads, s.head_dim).sum(axis=1)
    small = packed[taps + 2]
    at = heads + taps * 2 * state
    return (
        y,
        gx,
        grad_bc,
        gdt,
        small[:heads],
        grad_skip,
        packed[:taps],
        packed[taps],
        small[heads:at].reshape(taps, 2 * state),
        small[at : at + 2 * state],
    )


def solution(mesh):
    rows, both = P(("groups", "ctx"), "head"), P(("groups", "head"))
    return jax.shard_map(
        functools.partial(local, mesh.shape["ctx"]),
        mesh=mesh,
        in_specs=(rows, P(("groups", "ctx"), None), rows, P("head"), P("head"), P(None, "head"), P("head"), P(), P(), rows),
        out_specs=(rows, rows, P(("groups", "ctx"), None), rows, both, both, P("groups", "head"), both, P("groups", None), P("groups")),
        check_vma=False,
    )
```

```python
import functools

import jax
import jax.numpy as jnp
from jax import lax
from jax.experimental import pallas as pl
from jax.experimental.pallas import tpu as pltpu
from jax.sharding import PartitionSpec as P

F32, BF16 = jnp.float32, jnp.bfloat16
EXACT = lax.Precision.HIGHEST
LANES = 128
HALO = 8
GROUP = 4


def dot(a, b, ca=1, cb=0, precision=None):
    dims = (((ca,), (cb,)), ((), ()))
    return lax.dot_general(a, b, dims, preferred_element_type=F32, precision=precision)


def iota(shape, dim):
    return lax.broadcasted_iota(jnp.int32, shape, dim)


def lower_ones(size):
    return (iota((size, size), 0) >= iota((size, size), 1)).astype(F32)


def upper_ones(size):
    return (iota((size, size), 0) <= iota((size, size), 1)).astype(F32)


def sigmoid(v):
    return 1.0 / (1.0 + jnp.exp(-v))


def cols(start):
    return pl.ds(pl.multiple_of(start, LANES), LANES)


class Part:
    def __init__(self, rows, state, head_dim, base, chunks):
        self.rows, self.state, self.head_dim, self.base, self.chunks = rows, state, head_dim, base, chunks
        self.lane_width = chunks * LANES
        self.width = GROUP * self.lane_width
        self.per_chunk = LANES // head_dim
        self.lane_heads = chunks * self.per_chunk
        self.heads = GROUP * self.lane_heads
        self.head0 = base // head_dim
        self.span = slice(base, base + self.width)
        self.head_span = slice(self.head0, self.head0 + self.heads)


def lane_slices(s, value, scratch):
    for lane in range(GROUP):
        at = s.head0 + lane * s.lane_heads
        scratch[lane, :, 0 : s.lane_heads] = value[:, at : at + s.lane_heads]


def lane_join(s, scratch):
    return jnp.concatenate([scratch[lane][:, 0 : s.lane_heads] for lane in range(GROUP)], axis=1)


def spread(s, value, chunk):
    rows = value.shape[0]
    lane = iota((rows, LANES), 1)
    out = None
    for i in range(s.per_chunk):
        h = chunk * s.per_chunk + i
        col = jnp.broadcast_to(value[:, h : h + 1], (rows, LANES))
        out = col if out is None else jnp.where(lane >= i * s.head_dim, col, out)
    return out


def head_sums(s, value, chunk):
    r, c = iota((LANES, LANES), 0), iota((LANES, LANES), 1)
    one = (c == chunk * s.per_chunk + r // s.head_dim).astype(F32).astype(BF16)
    hi = value.astype(BF16)
    lo = (value - hi.astype(F32)).astype(BF16)
    return dot(jnp.concatenate([hi, lo], axis=1), jnp.concatenate([one, one], axis=0))


def decay(step_t, alog_t):
    rate = -step_t * jnp.exp(alog_t)
    return rate, dot(rate, upper_ones(step_t.shape[1]), precision=EXACT)


def decay_factors(step_t, alog_t):
    _, cum = decay(step_t, alog_t)
    rows = step_t.shape[1]
    last = cum[:, rows - 1 : rows]
    return jnp.transpose(jnp.exp(cum)), jnp.transpose(jnp.exp(last - cum) * step_t), jnp.transpose(cum)


def conv_into(buf, halo, x, weight, bias):
    rows = x.shape[0]
    buf[0:HALO, :] = halo.astype(F32)
    buf[HALO : HALO + rows, :] = x.astype(F32)
    taps = weight.shape[0]
    total = jnp.broadcast_to(bias, x.shape)
    for k in range(taps):
        first = HALO - (taps - 1) + k
        total = total + weight[k : k + 1, :] * buf[first : first + rows, :]
    return total


def states_kernel(s, first, lane_ref, x_hbm, g_hbm, halo_ref, dtt_ref, alt_ref, wx_ref, bx_ref, *rest):
    if first:
        bc_ref, wbc_ref, bbc_ref, mbc_ref, *rest = rest
    else:
        mbc_ref, *rest = rest
    x_ref, g_ref, mx_ref, wxs_ref, ges_ref = rest[:5]
    outs = rest[5 : 5 + GROUP]
    msg, endw_s, ecum_s, xbuf, *bbuf, in_sems = rest[5 + GROUP :]
    me = lane_ref[0]
    loads = [
        pltpu.make_async_copy(x_hbm.at[:, s.span], x_ref, in_sems.at[0]),
        pltpu.make_async_copy(g_hbm.at[:, s.span], g_ref, in_sems.at[1]),
    ]
    for c in loads:
        c.start()
    grow, shrink, cum = decay_factors(dtt_ref[...], alt_ref[...])
    lane_slices(s, shrink, endw_s)
    lane_slices(s, grow, ecum_s)
    total8 = jnp.broadcast_to(grow[s.rows - 1 : s.rows, s.head_span], (8, s.heads))
    if first:
        width = x_hbm.shape[1]
        v = conv_into(bbuf[0], halo_ref[:, width:], bc_ref[...], wbc_ref[...], bbc_ref[...])
        mbc_ref[...] = (v * sigmoid(v)).astype(BF16)
    mixed_bc = mbc_ref[...].astype(F32)
    b_t = jnp.transpose(mixed_bc[:, : s.state]).astype(BF16)
    c_t = jnp.transpose(mixed_bc[:, s.state :]).astype(BF16)
    for c in loads:
        c.wait()

    def lane_body(lane, carry):
        base = lane * s.lane_width
        for c in range(s.chunks):
            at = cols(base + c * LANES)
            wide = cols(s.base + base + c * LANES)
            v = conv_into(xbuf.at[c], halo_ref[:, wide], x_ref[:, at], wx_ref[:, wide], bx_ref[:, wide])
            mixed = (v * sigmoid(v)).astype(BF16)
            mx_ref[:, at] = mixed
            wxs_ref[:, at] = (mixed.astype(F32) * spread(s, endw_s[lane], c)).astype(BF16)
            ges_ref[:, at] = (g_ref[:, at].astype(F32) * spread(s, ecum_s[lane], c)).astype(BF16)
        whole = pl.ds(pl.multiple_of(base, LANES), s.lane_width)
        rows = slice(0, s.state)
        msg[lane, rows, : s.lane_width] = dot(b_t, wxs_ref[:, whole]).astype(BF16)
        msg[lane, rows, s.lane_width :] = dot(c_t, ges_ref[:, whole]).astype(BF16)
        shape = (s.heads, s.lane_width)
        pick = (iota(shape, 0) == lane * s.lane_heads + iota(shape, 1) // s.head_dim).astype(F32)
        total = dot(total8, pick, precision=EXACT)
        hi = total.astype(BF16).astype(F32)
        mid = (total - hi).astype(BF16).astype(F32)
        low = total - hi - mid
        row = iota(total.shape, 0)
        parts = jnp.where(row == 0, hi, jnp.where(row == 1, mid, jnp.where(row == 2, low, 0.0)))
        msg[lane, s.state : s.state + 8, : s.lane_width] = parts.astype(BF16)
        msg[lane, s.state : s.state + 8, s.lane_width :] = parts.astype(BF16)
        return carry

    lax.fori_loop(0, GROUP, lane_body, 0)
    for d in range(GROUP):
        outs[d][...] = msg[me ^ d]


def intra_kernel(s, first, x_ref, g_ref, mx_ref, mbc_ref, halo_ref, dtt_ref, alt_ref, dsk_ref, wx_ref, bx_ref, *rest):
    if first:
        y_ref, dx_ref, slope_ref, grow_ref, shrink_ref, rs_ref, vs_ref, ds_ref, *rest = rest
    else:
        ds_in, y_ref, dx_ref, slope_ref, grow_ref, shrink_ref, rs_ref, vs_ref, dbc_ref, *rest = rest
    cum_s, ecum_s, endw_s, cumt_s, dtt_s, rs_s, vs_s, xbuf = rest
    rows = s.rows
    grow, shrink, cum = decay_factors(dtt_ref[...], alt_ref[...])
    lane_slices(s, cum, cum_s)
    lane_slices(s, grow, ecum_s)
    lane_slices(s, shrink, endw_s)
    _, cum_t = decay(dtt_ref[...], alt_ref[...])
    for lane in range(GROUP):
        at = s.head0 + lane * s.lane_heads
        cumt_s[lane, 0 : s.lane_heads, :] = cum_t[at : at + s.lane_heads, :]
        dtt_s[lane, 0 : s.lane_heads, :] = dtt_ref[at : at + s.lane_heads, :]
    b, c_m = mbc_ref[:, : s.state], mbc_ref[:, s.state :]
    causal = iota((rows, rows), 0) >= iota((rows, rows), 1)
    scores = jnp.where(causal, dot(c_m, b, 1, 1), 0.0)
    lane_id = iota((rows, LANES), 1)
    masks = [((lane_id >= i * s.head_dim) & (lane_id < (i + 1) * s.head_dim)).astype(F32).astype(BF16) for i in range(s.per_chunk)]

    def lane_body(lane, d_scores):
        base = lane * s.lane_width
        row_acc = jnp.zeros((rows, LANES), F32)
        col_acc = jnp.zeros((rows, LANES), F32)
        cum_l = cum_s[lane]
        for c in range(s.chunks):
            at = cols(base + c * LANES)
            wide = cols(s.base + base + c * LANES)
            x, g = mx_ref[:, at], g_ref[:, at]
            x_st = jnp.concatenate([x * m for m in masks], axis=0)
            g_st = jnp.concatenate([g * m for m in masks], axis=0)
            d_mix = dot(g_st, x, 1, 1)
            mixes = []
            for i in range(s.per_chunk):
                h = c * s.per_chunk + i
                gap = jnp.broadcast_to(cum_l[:, h : h + 1], (rows, rows)) - cumt_s[lane, h : h + 1, :]
                e = jnp.exp(jnp.minimum(gap, 0.0)) * dtt_s[lane, h : h + 1, :]
                mixes.append((e * scores).astype(BF16))
                d_scores = d_scores + d_mix[i * rows : (i + 1) * rows, :] * e
            y = dot(jnp.concatenate(mixes, axis=1), x_st)
            dx = dot(jnp.concatenate(mixes, axis=0), g_st, 0, 0)
            xf, gf, skip = x.astype(F32), g.astype(F32), dsk_ref[:, wide]
            row_acc = row_acc + head_sums(s, gf * y, c)
            col_acc = col_acc + head_sums(s, xf * dx, c)
            y_ref[:, at] = (y + skip * xf).astype(BF16)
            dx_ref[:, at] = (dx + skip * gf).astype(BF16)
            grow_ref[:, at] = spread(s, ecum_s[lane], c)
            shrink_ref[:, at] = spread(s, endw_s[lane], c)
            v = conv_into(xbuf.at[c], halo_ref[:, wide], x_ref[:, at], wx_ref[:, wide], bx_ref[:, wide])
            slope_ref[:, at] = silu_slope(v)
        rs_s[lane] = row_acc
        vs_s[lane] = col_acc
        return d_scores

    start = jnp.zeros((rows, rows), F32) if first else ds_in[...]
    d_scores = lax.fori_loop(0, GROUP, lane_body, start)
    rs_ref[...] = lane_join(s, rs_s)
    vs_ref[...] = lane_join(s, vs_s)
    if first:
        ds_ref[...] = d_scores
    else:
        d_scores = jnp.where(causal, d_scores, 0.0).astype(BF16)
        dbc_ref[:, : s.state] = dot(d_scores, c_m, 0, 0)
        dbc_ref[:, s.state :] = dot(d_scores, b)


def place_blocks(me, srcs, buf):
    for d in range(GROUP):
        buf[me ^ d] = srcs[d][...]


def total_row(s, buf, i, at):
    return jnp.sum(buf[i, s.state : s.state + 8, at].astype(F32), axis=0, keepdims=True)


def group_sum_kernel(s, pair, at_ref, *refs):
    srcs, buf = refs[:GROUP], refs[-1]
    outs = refs[GROUP:-1]
    me, high = at_ref[0], at_ref[1]
    place_blocks(me, srcs, buf)
    for c in range(s.chunks):
        at = slice(c * LANES, (c + 1) * LANES)
        at_r = slice(s.lane_width + c * LANES, s.lane_width + (c + 1) * LANES)
        totals = [total_row(s, buf, i, at) for i in range(GROUP)]
        ahead = jnp.zeros((s.state, LANES), F32)
        back = jnp.zeros((s.state, LANES), F32)
        every = jnp.ones((1, LANES), F32)
        for i in range(GROUP):
            ahead = totals[i] * ahead + buf[i, 0 : s.state, at].astype(F32)
            r = GROUP - 1 - i
            back = totals[r] * back + buf[r, 0 : s.state, at_r].astype(F32)
            every = every * totals[i]
        if pair:
            outs[0][:, at] = jnp.where(high == 0, ahead, back).astype(BF16)
        else:
            outs[0][:, at] = ahead.astype(BF16)
            outs[1][:, at] = back.astype(BF16)
            outs[2][:, at] = jnp.broadcast_to(every, (8, LANES))


def group_scan_kernel(s, pair, at_ref, *refs):
    srcs = refs[:GROUP]
    n_in = 1 if pair else 2
    before = refs[GROUP : GROUP + n_in]
    outs = refs[GROUP + n_in : 2 * GROUP + n_in]
    buf, done = refs[2 * GROUP + n_in :]
    me, high = at_ref[0], at_ref[1]
    place_blocks(me, srcs, buf)
    for c in range(s.chunks):
        at = slice(c * LANES, (c + 1) * LANES)
        at_r = slice(s.lane_width + c * LANES, s.lane_width + (c + 1) * LANES)
        totals = [total_row(s, buf, i, at) for i in range(GROUP)]
        first = before[0][:, at].astype(F32)
        if pair:
            ahead = jnp.where(high == 1, first, 0.0)
            back = jnp.where(high == 0, first, 0.0)
        else:
            ahead, back = first, before[1][:, at].astype(F32)
        for i in range(GROUP):
            done[i, :, at] = ahead.astype(BF16)
            r = GROUP - 1 - i
            done[r, :, at_r] = back.astype(BF16)
            if i < GROUP - 1:
                ahead = totals[i] * ahead + buf[i, 0 : s.state, at].astype(F32)
                back = totals[r] * back + buf[r, 0 : s.state, at_r].astype(F32)
    for d in range(GROUP):
        outs[d][...] = done[me ^ d]


def conv_back(buf, dv, weight):
    rows, taps = dv.shape[0], weight.shape[0]
    zeros = jnp.zeros((HALO, dv.shape[1]), F32)
    buf[0:HALO, :] = zeros
    buf[HALO : HALO + rows, :] = dv
    buf[HALO + rows : 2 * HALO + rows, :] = zeros
    own = before = None
    for k in range(taps):
        w = weight[k : k + 1, :]
        first = HALO + taps - 1 - k
        part = w * buf[first : first + rows, :]
        own = part if own is None else own + part
        first = taps - 1 - k
        part = w * buf[first : first + HALO, :]
        before = part if before is None else before + part
    keep = iota(before.shape, 0) >= HALO - (taps - 1)
    return own, jnp.where(keep, before, 0.0)


def conv_weight_rows(buf, dv, taps):
    rows = dv.shape[0]
    out = []
    for k in range(taps):
        first = HALO - (taps - 1) + k
        out.append(jnp.sum(dv * buf[first : first + rows, :], axis=0, keepdims=True))
    out.append(jnp.sum(dv, axis=0, keepdims=True))
    return out


def silu_slope(v):
    sig = sigmoid(v)
    return sig * (1.0 + v * (1.0 - sig))


def pair_grads_kernel(s, lane_ref, wxs_ref, ges_ref, dbc_in, *rest):
    srcs, (dbc_ref, held) = rest[:GROUP], rest[GROUP:]
    place_blocks(lane_ref[0], srcs, held)
    d_b, d_c = dbc_in[:, : s.state], dbc_in[:, s.state :]
    for lane in range(GROUP):
        whole = slice(lane * s.lane_width, (lane + 1) * s.lane_width)
        d_c = d_c + dot(ges_ref[:, whole], held[lane, :, : s.lane_width], 1, 1)
        d_b = d_b + dot(wxs_ref[:, whole], held[lane, :, s.lane_width :], 1, 1)
    dbc_ref[:, : s.state] = d_b.astype(dbc_ref.dtype)
    dbc_ref[:, s.state :] = d_c.astype(dbc_ref.dtype)


def outputs_kernel(s, first, lane_ref, x_ref, g_ref, mx_ref, wxs_ref, ges_ref, mbc_ref, halo_ref, wx_ref, yl_ref, dxl_ref, slope_ref, grow_ref, shrink_ref, *rest):
    srcs, rest = rest[:GROUP], rest[GROUP:]
    if not first:
        rest = rest[2:]
    y_hbm, gx_hbm, gxt_ref, ho_ref, pk_ref, rs_ref, us_ref, hl_ref = rest[:8]
    held, y_s, gx_s, xbuf, dbuf, rs_s, us_s, hl_s, out_sems = rest[8:]
    place_blocks(lane_ref[0], srcs, held)
    rows, taps = s.rows, wx_ref.shape[0]
    b, c_m = mbc_ref[:, : s.state], mbc_ref[:, s.state :]
    shape = (s.lane_width, LANES)
    pick = (iota(shape, 0) // s.head_dim == iota(shape, 1)).astype(F32)

    def lane_body(lane, carry):
        base = lane * s.lane_width
        row_acc = jnp.zeros((rows, LANES), F32)
        col_acc = jnp.zeros((rows, LANES), F32)
        links = []
        for c in range(s.chunks):
            at = cols(base + c * LANES)
            wide = cols(s.base + base + c * LANES)
            state = held[lane, :, c * LANES : (c + 1) * LANES]
            later = held[lane, :, s.lane_width + c * LANES : s.lane_width + (c + 1) * LANES]
            y = dot(c_m, state)
            row_acc = row_acc + head_sums(s, ges_ref[:, at].astype(F32) * y, c)
            y_s[:, at] = (yl_ref[:, at].astype(F32) + y * grow_ref[:, at]).astype(BF16)
            dx = dot(b, later)
            col_acc = col_acc + head_sums(s, wxs_ref[:, at].astype(F32) * dx, c)
            links.append(jnp.sum(state.astype(F32) * later.astype(F32), axis=0, keepdims=True))
            weight = wx_ref[:, wide]
            dv = (dxl_ref[:, at].astype(F32) + dx * shrink_ref[:, at]) * slope_ref[:, at]
            own, before = conv_back(dbuf.at[c], dv, weight)
            gx_s[:, at] = own.astype(BF16)
            gxt_ref[:, at] = own[rows - HALO :, :]
            ho_ref[:, at] = before.astype(BF16)
            buf = xbuf.at[c]
            buf[0:HALO, :] = halo_ref[:, wide].astype(F32)
            buf[HALO : HALO + rows, :] = x_ref[:, at].astype(F32)
            packed = conv_weight_rows(buf, dv, taps)
            packed.append(jnp.sum(g_ref[:, at].astype(F32) * mx_ref[:, at].astype(F32), axis=0, keepdims=True))
            packed.append(jnp.zeros((8 - len(packed), LANES), F32))
            pk_ref[:, at] = jnp.concatenate(packed, axis=0)
        rs_s[lane] = row_acc
        us_s[lane] = col_acc
        whole = pl.ds(pl.multiple_of(base, LANES), s.lane_width)
        skip = pk_ref[:, whole]
        link = jnp.broadcast_to(jnp.concatenate(links, axis=1), skip.shape)
        row = iota(skip.shape, 0)
        hl_s[lane] = dot(jnp.where(row == 0, link, skip), pick, precision=EXACT)
        return carry

    lax.fori_loop(0, GROUP, lane_body, 0)
    stores = [
        pltpu.make_async_copy(y_s, y_hbm.at[:, s.span], out_sems.at[0]),
        pltpu.make_async_copy(gx_s, gx_hbm.at[:, s.span], out_sems.at[1]),
    ]
    for c in stores:
        c.start()
    rs_ref[...] = lane_join(s, rs_s)
    us_ref[...] = lane_join(s, us_s)
    hl_ref[...] = lane_join(s, hl_s)
    for c in stores:
        c.wait()


def tail_kernel(parts, bc_ref, halo_ref, dtt_ref, alt_ref, wbc_ref, bbc_ref, dbc_ref, dbc_other, *rest):
    n = len(parts)
    groups, rest = [rest[i * 7 : (i + 1) * 7] for i in range(n)], rest[7 * n :]
    gdt_ref, pk_ref, back_ref, gbc_ref, bbuf, dbuf = rest
    taps, rows = wbc_ref.shape[0], bc_ref.shape[0]
    join = lambda i: jnp.concatenate([g[i][...] for g in groups], axis=1)
    rate, cum = decay(dtt_ref[...], alt_ref[...])
    inter = jnp.transpose(join(3))
    through = jnp.transpose(join(1)) + inter
    d_cum = jnp.transpose(join(0) + join(2)) - through
    link = join(4)
    heads = rate.shape[0]
    sums = jnp.transpose(link)
    d_last = jnp.sum(inter, axis=1, keepdims=True) + jnp.exp(cum[:, rows - 1 : rows]) * sums[:, 0:1]
    d_cum = d_cum + jnp.where(iota(d_cum.shape, 1) == rows - 1, d_last, 0.0)
    d_rate = dot(d_cum, lower_ones(rows), precision=EXACT)
    step = dtt_ref[...]
    gdt_ref[...] = through / step - jnp.exp(alt_ref[...]) * d_rate
    gal = jnp.broadcast_to(jnp.sum(rate * d_rate, axis=1, keepdims=True), (heads, LANES))
    gal = jnp.transpose(gal)[0:1, :]

    width = halo_ref.shape[1] - bc_ref.shape[1]
    v = conv_into(bbuf, halo_ref[:, width:], bc_ref[...], wbc_ref[...], bbc_ref[...])
    dv = (dbc_ref[...].astype(F32) + dbc_other[...].astype(F32)) * silu_slope(v)
    own, before = conv_back(dbuf, dv, wbc_ref[...])
    gbc_ref[...] = own
    bc_rows = conv_weight_rows(bbuf, dv, taps)
    pk_ref[...] = jnp.zeros(pk_ref.shape, pk_ref.dtype)
    for s, g in zip(parts, groups):
        pk_ref[0 : taps + 1, s.span] = g[5][0 : taps + 1, :].astype(BF16)
        back_ref[:, s.span] = g[6][...]
    back_ref[:, width:] = before.astype(BF16)
    row = taps + 1
    pk_ref[row : row + 1, 0:heads] = gal.astype(BF16)
    pk_ref[row : row + 1, LANES : LANES + heads] = link[row : row + 1, :].astype(BF16)
    for k, r in enumerate(bc_rows):
        at = 2 * LANES + k * r.shape[1]
        pk_ref[row : row + 1, at : at + r.shape[1]] = r.astype(BF16)


def finish_kernel(parts, taps, heads, gx_in, pk_ref, other_ref, back_ref, gbc_ref, *rest):
    n = len(parts)
    tails, rest = rest[:n], rest[n:]
    gx_hbm, grad_bc, gwx_ref, gwbc_ref, small_ref, gxt, sem = rest
    rows = gbc_ref.shape[0]
    width = gxt.shape[1]
    for s, t in zip(parts, tails):
        gxt[:, s.span] = (t[...] + back_ref[:, s.span].astype(F32)).astype(BF16)
    store = pltpu.make_async_copy(gxt, gx_hbm.at[rows - HALO : rows, :], sem)
    store.start()
    grad_bc[...] = gbc_ref[...].astype(BF16)
    tail = gbc_ref[rows - HALO : rows, :] + back_ref[:, width:].astype(F32)
    grad_bc[rows - HALO : rows, :] = tail.astype(BF16)
    total = pk_ref[...].astype(F32) + other_ref[...].astype(F32)
    gwx_ref[...] = total[0:taps, :]
    bc_width = gbc_ref.shape[1]
    row = total[taps + 1 : taps + 2, :]
    for k in range(taps):
        at = 2 * LANES + k * bc_width
        gwbc_ref[k : k + 1, :] = row[:, at : at + bc_width]
    small_ref[...] = total[taps : taps + 2, :]
    store.wait()


VMEM = pl.BlockSpec(memory_space=pltpu.VMEM)
SMEM = pl.BlockSpec(memory_space=pltpu.SMEM)
ANY = pl.BlockSpec(memory_space=pl.ANY)
HBM = pl.BlockSpec(memory_space=pltpu.HBM)


def call(kernel, name, args, in_specs, outs, out_specs, scratch, flops=0, after=(), aliases=None):
    n, extra = len(args), len(after)

    def body(*refs):
        kernel(*refs[:n], *refs[n + extra :])

    moved = sum(a.size * a.dtype.itemsize for a in (*args, *outs))
    return pl.pallas_call(
        body,
        name=name,
        out_shape=tuple(outs),
        in_specs=list(in_specs) + [ANY] * extra,
        out_specs=tuple(out_specs),
        scratch_shapes=scratch,
        input_output_aliases=aliases or {},
        compiler_params=pltpu.CompilerParams(vmem_limit_bytes=32 << 20),
        cost_estimate=pl.CostEstimate(flops=flops, bytes_accessed=moved, transcendentals=0),
    )(*args, *after)


def shift(value, count, steps):
    pairs = [(i, i + steps) for i in range(count) if 0 <= i + steps < count]
    return lax.ppermute(value, "ctx", pairs)


def swap(value, count, mask):
    return lax.ppermute(value, "ctx", [(i, i ^ mask) for i in range(count)])


def group_scan(ahead, back, every, count):
    found = []
    for sign, value in ((1, ahead), (-1, back)):
        total = shift(every, count, sign * GROUP)
        value = shift(value, count, sign * GROUP).astype(F32)
        step = GROUP
        while step < count:
            value = value + total[0:1] * shift(value.astype(BF16), count, sign * step).astype(F32)
            total = total * shift(total, count, sign * step)
            step *= 2
        found.append(value.astype(BF16))
    return found


def local(n_ctx, x_in, bc_in, step_dt, a_log, d_skip, conv_wx, conv_bx, conv_wbc, conv_bbc, grad_out):
    rows, width = x_in.shape
    heads, state = step_dt.shape[1], bc_in.shape[1] // 2
    head_dim = width // heads
    taps = conv_wx.shape[0]
    n_chunks = width // (GROUP * LANES)
    cut = (n_chunks + 1) // 2
    parts = [Part(rows, state, head_dim, 0, cut), Part(rows, state, head_dim, cut * GROUP * LANES, n_chunks - cut)]
    pair = n_ctx == 2 * GROUP
    index = lax.axis_index("ctx")
    place = jnp.stack([index % GROUP, index // GROUP]).astype(jnp.int32)
    sds = jax.ShapeDtypeStruct
    vm = pltpu.VMEM

    halo = shift(jnp.concatenate([x_in[-HALO:], bc_in[-HALO:]], axis=1), n_ctx, 1)
    step_t, al_t, bx, bbc = step_dt.T, a_log[:, None], conv_bx[None, :], conv_bbc[None, :]
    msg_rows = state + 8
    per_head = vm((GROUP, rows, LANES), F32)
    sems2 = pltpu.SemaphoreType.DMA((2,))
    bc_shape = (rows, 2 * state)

    def states(s, first, extra, after=()):
        args = (place, x_in, grad_out, halo, step_t, al_t, conv_wx, bx, *extra)
        wide = sds((rows, s.width), BF16)
        msgs = [sds((msg_rows, 2 * s.lane_width), BF16)] * GROUP
        return call(
            functools.partial(states_kernel, s, first),
            "states",
            args,
            [SMEM, HBM, HBM] + [VMEM] * (len(args) - 3),
            ([sds(bc_shape, BF16)] if first else []) + [wide] * 5 + msgs,
            [VMEM] * (6 if first else 5) + [VMEM] * GROUP,
            [vm((GROUP, msg_rows, 2 * s.lane_width), BF16), per_head, per_head, vm((s.chunks, rows + HALO, LANES), F32)]
            + ([vm((rows + HALO, 2 * state), F32)] if first else [])
            + [sems2],
            4 * rows * s.width * state,
            after,
        )

    def exchange(messages):
        return [messages[0]] + [swap(messages[d], n_ctx, d) for d in range(1, GROUP)]

    def intra(s, first, wide, d_scores, after=()):
        x, g, mx = wide[:3]
        args = (x, g, mx, mbc, halo, step_t, al_t, skip_wide, conv_wx, bx) + (() if first else (d_scores,))
        per_row = vm((GROUP, 16, rows), F32)
        return call(
            functools.partial(intra_kernel, s, first),
            "intra",
            args,
            [VMEM] * len(args),
            [sds((rows, s.width), BF16)] * 2
            + [sds((rows, s.width), F32)] * 3
            + [sds((rows, s.heads), F32)] * 2
            + [sds((rows, rows) if first else bc_shape, F32)],
            [VMEM] * 8,
            [per_head, per_head, per_head, per_row, per_row, per_head, per_head, vm((s.chunks, rows + HALO, LANES), F32)],
            12 * rows * s.width * rows,
            after,
        )

    def sums(s, blocks, after=()):
        shape = (state, s.lane_width)
        outs = [sds(shape, BF16)] if pair else [sds(shape, BF16)] * 2 + [sds((8, s.lane_width), F32)]
        summed = call(
            functools.partial(group_sum_kernel, s, pair),
            "group_sum",
            (place, *blocks),
            [SMEM] + [VMEM] * GROUP,
            outs,
            [VMEM] * len(outs),
            [vm((GROUP, msg_rows, 2 * s.lane_width), BF16)],
            state * s.width,
            after,
        )
        return [swap(summed[0], n_ctx, GROUP)] if pair else group_scan(*summed, n_ctx)

    def scan(s, blocks, before, after=()):
        return call(
            functools.partial(group_scan_kernel, s, pair),
            "group_scan",
            (place, *blocks, *before),
            [SMEM] + [VMEM] * GROUP + [VMEM] * len(before),
            [sds((state, 2 * s.lane_width), BF16)] * GROUP,
            [VMEM] * GROUP,
            [vm((GROUP, msg_rows, 2 * s.lane_width), BF16), vm((GROUP, state, 2 * s.lane_width), BF16)],
            state * s.width,
            after,
        )

    def pair_grads(s, wide, dbc, held, dtype, after=()):
        return call(
            functools.partial(pair_grads_kernel, s),
            "pair_grads",
            (place, wide[3], wide[4], dbc, *held),
            [SMEM] + [VMEM] * 3 + [VMEM] * GROUP,
            [sds(bc_shape, dtype)],
            [VMEM],
            [vm((GROUP, state, 2 * s.lane_width), BF16)],
            4 * rows * s.width * state,
            after,
        )[0]

    def outputs(s, first, wide, inner, held, whole, after=()):
        args = (place, *wide, mbc, halo, conv_wx, *inner[:5], *held, *whole)
        return call(
            functools.partial(outputs_kernel, s, first),
            "outputs",
            args,
            [SMEM] + [VMEM] * 13 + [VMEM] * GROUP + [HBM] * len(whole),
            [sds((rows, width), BF16)] * 2
            + [sds((HALO, s.width), F32), sds((HALO, s.width), BF16), sds((8, s.width), F32)]
            + [sds((rows, s.heads), F32)] * 2
            + [sds((8, s.heads), F32)],
            [HBM, HBM] + [VMEM] * 6,
            [
                vm((GROUP, state, 2 * s.lane_width), BF16),
                vm((rows, s.width), BF16),
                vm((rows, s.width), BF16),
                vm((s.chunks, rows + HALO, LANES), F32),
                vm((s.chunks, rows + 2 * HALO, LANES), F32),
                per_head,
                per_head,
                vm((GROUP, 8, LANES), F32),
                sems2,
            ],
            4 * rows * s.width * state,
            after,
            {} if first else {14 + GROUP: 0, 15 + GROUP: 1},
        )

    a, b = parts
    skip_wide = jnp.repeat(d_skip, head_dim)[None, :]
    mbc, *rest = states(a, True, (bc_in, conv_wbc, bbc))
    wide_a, msgs = rest[:5], rest[5:]
    blocks_a = exchange(msgs)
    rest = states(b, False, (mbc,))
    wide_b, msgs = rest[:5], rest[5:]
    blocks_b = exchange(msgs)
    inner_a = intra(a, True, wide_a, None, (msgs[0],))
    before_a = sums(a, blocks_a, (inner_a[-1],))
    before_b = sums(b, blocks_b)
    inner_b = intra(b, False, wide_b, inner_a[-1])
    held_a = exchange(scan(a, blocks_a, before_a, (inner_b[-1],)))
    held_b = exchange(scan(b, blocks_b, before_b))
    dbc = pair_grads(a, wide_a, inner_b[-1], held_a, F32)
    out_a = outputs(a, True, wide_a, inner_a, held_a, ())
    dbc = pair_grads(b, wide_b, dbc, held_b, BF16, (out_a[-1],))
    n_head = lax.axis_size("head")
    if n_head == 2:
        other = lax.ppermute(dbc, "head", [(0, 1), (1, 0)])
    else:
        other = (lax.psum(dbc.astype(F32), "head") - dbc.astype(F32)).astype(BF16)
    out_b = outputs(b, False, wide_b, inner_b, held_b, out_a[:2])
    y, gx = out_b[:2]

    args = [bc_in, halo, step_t, al_t, conv_wbc, bbc, dbc, other]
    for inner, out in ((inner_a, out_a), (inner_b, out_b)):
        args += [inner[5], inner[6], out[5], out[6], out[7], out[4], out[3]]
    gdt_t, packed, back, gbc = call(
        functools.partial(tail_kernel, parts),
        "tail",
        tuple(args),
        [VMEM] * len(args),
        [sds((heads, rows), F32), sds((8, width), BF16), sds((HALO, width + 2 * state), BF16), sds(bc_shape, F32)],
        [VMEM] * 4,
        [vm((rows + HALO, 2 * state), F32), vm((rows + 2 * HALO, 2 * state), F32)],
    )
    back = shift(back, n_ctx, -1)
    step = 1
    while 2 * step < n_ctx:
        packed = packed + swap(packed, n_ctx, step)
        step *= 2
    last = swap(packed, n_ctx, step)
    args = (gx, packed, last, back, gbc, out_a[2], out_b[2])
    gx, grad_bc, gwx, gwbc, small = call(
        functools.partial(finish_kernel, parts, taps, heads),
        "finish",
        args,
        [HBM] + [VMEM] * (len(args) - 1),
        [sds((rows, width), BF16), sds(bc_shape, BF16), sds((taps, width), F32), sds((taps, 2 * state), F32), sds((2, width), F32)],
        [HBM] + [VMEM] * 4,
        [vm((HALO, width), BF16), pltpu.SemaphoreType.DMA],
        aliases={0: 0},
    )
    at = 2 * LANES + taps * 2 * state
    return (
        y,
        gx,
        grad_bc,
        gdt_t.T,
        small[1, :heads],
        small[1, LANES : LANES + heads],
        gwx,
        small[0],
        gwbc,
        small[1, at : at + 2 * state],
    )


def solution(mesh):
    rows, both = P(("groups", "ctx"), "head"), P(("groups", "head"))
    return jax.shard_map(
        functools.partial(local, mesh.shape["ctx"]),
        mesh=mesh,
        in_specs=(rows, P(("groups", "ctx"), None), rows, P("head"), P("head"), P(None, "head"), P("head"), P(), P(), rows),
        out_specs=(rows, rows, P(("groups", "ctx"), None), rows, both, both, P("groups", "head"), both, P("groups", None), P("groups")),
        check_vma=False,
    )
```

```python
import functools

import jax
import jax.numpy as jnp
from jax import lax
from jax.experimental import pallas as pl
from jax.experimental.pallas import tpu as pltpu
from jax.sharding import PartitionSpec as P

F32, BF16 = jnp.float32, jnp.bfloat16
EXACT = lax.Precision.HIGHEST
LANES = 128
HALO = 8
GROUP = 4


def dot(a, b, ca=1, cb=0, precision=None):
    dims = (((ca,), (cb,)), ((), ()))
    return lax.dot_general(a, b, dims, preferred_element_type=F32, precision=precision)


def iota(shape, dim):
    return lax.broadcasted_iota(jnp.int32, shape, dim)


def lower_ones(size):
    return (iota((size, size), 0) >= iota((size, size), 1)).astype(F32)


def upper_ones(size):
    return (iota((size, size), 0) <= iota((size, size), 1)).astype(F32)


def sigmoid(v):
    return 1.0 / (1.0 + jnp.exp(-v))


def cols(start):
    return pl.ds(pl.multiple_of(start, LANES), LANES)


class Part:
    def __init__(self, rows, state, head_dim, base, chunks):
        self.rows, self.state, self.head_dim, self.base, self.chunks = rows, state, head_dim, base, chunks
        self.lane_width = chunks * LANES
        self.width = GROUP * self.lane_width
        self.per_chunk = LANES // head_dim
        self.lane_heads = chunks * self.per_chunk
        self.heads = GROUP * self.lane_heads
        self.head0 = base // head_dim
        self.span = slice(base, base + self.width)
        self.head_span = slice(self.head0, self.head0 + self.heads)


def lane_slices(s, value, scratch):
    for lane in range(GROUP):
        at = s.head0 + lane * s.lane_heads
        scratch[lane, :, 0 : s.lane_heads] = value[:, at : at + s.lane_heads]


def lane_join(s, scratch):
    return jnp.concatenate([scratch[lane][:, 0 : s.lane_heads] for lane in range(GROUP)], axis=1)


def spread(s, value, chunk):
    rows = value.shape[0]
    lane = iota((rows, LANES), 1)
    out = None
    for i in range(s.per_chunk):
        h = chunk * s.per_chunk + i
        col = jnp.broadcast_to(value[:, h : h + 1], (rows, LANES))
        out = col if out is None else jnp.where(lane >= i * s.head_dim, col, out)
    return out


def head_sums(s, value, chunk):
    r, c = iota((LANES, LANES), 0), iota((LANES, LANES), 1)
    one = (c == chunk * s.per_chunk + r // s.head_dim).astype(F32).astype(BF16)
    hi = value.astype(BF16)
    lo = (value - hi.astype(F32)).astype(BF16)
    return dot(jnp.concatenate([hi, lo], axis=1), jnp.concatenate([one, one], axis=0))


def column(row):
    return jnp.transpose(jnp.broadcast_to(row, (8, row.shape[1])))[:, 0:1]


def decay(step_t, alog):
    rate = -step_t * jnp.exp(column(alog))
    return rate, dot(rate, upper_ones(step_t.shape[1]), precision=EXACT)


def decay_factors(step_t, alog):
    _, cum = decay(step_t, alog)
    rows = step_t.shape[1]
    last = cum[:, rows - 1 : rows]
    return jnp.transpose(jnp.exp(cum)), jnp.transpose(jnp.exp(last - cum) * step_t)


def conv_into(buf, halo, x, weight, bias):
    rows = x.shape[0]
    buf[0:HALO, :] = halo.astype(F32)
    buf[HALO : HALO + rows, :] = x.astype(F32)
    taps = weight.shape[0]
    total = jnp.broadcast_to(bias, x.shape)
    for k in range(taps):
        first = HALO - (taps - 1) + k
        total = total + weight[k : k + 1, :] * buf[first : first + rows, :]
    return total


def factors_kernel(parts, x_hbm, g_hbm, dtt_hbm, al_hbm, *refs):
    n = len(parts)
    outs, (dtt_ref, al_ref, ecum_s, sems) = [refs[3 * i : 3 * i + 3] for i in range(n)], refs[3 * n :]
    small = [
        pltpu.make_async_copy(dtt_hbm, dtt_ref, sems.at[2 * n]),
        pltpu.make_async_copy(al_hbm, al_ref, sems.at[2 * n + 1]),
    ]
    for c in small:
        c.start()
    loads = []
    for i, (s, out) in enumerate(zip(parts, outs)):
        loads.append(
            [
                pltpu.make_async_copy(g_hbm.at[:, s.span], out[1], sems.at[2 * i]),
                pltpu.make_async_copy(x_hbm.at[:, s.span], out[0], sems.at[2 * i + 1]),
            ]
        )
        for c in loads[-1]:
            c.start()
    for c in small:
        c.wait()
    grow, _ = decay_factors(dtt_ref[...], al_ref[...])
    for s, out, load in zip(parts, outs, loads):
        _, g_ref, ges_ref = out
        lane_slices(s, grow, ecum_s)

        load[0].wait()

        def scale_body(lane, carry):
            for c in range(s.chunks):
                at = cols(lane * s.lane_width + c * LANES)
                ges_ref[:, at] = (g_ref[:, at].astype(F32) * spread(s, ecum_s[lane], c)).astype(BF16)
            return carry

        lax.fori_loop(0, GROUP, scale_body, 0, unroll=True)
    for load in loads:
        load[1].wait()


def states_kernel(s, first, lane_ref, x_ref, ges_ref, dtt_ref, al_ref, halo_ref, wx_ref, bx_ref, *rest):
    if first:
        bc_ref, wbc_ref, bbc_ref, mbc_ref, *rest = rest
    else:
        mbc_ref, *rest = rest
    mx_ref, wxs_ref = rest[:2]
    outs = rest[2 : 2 + GROUP]
    msg, endw_s, xbuf, *bbuf = rest[2 + GROUP :]
    me = lane_ref[0]
    grow, shrink = decay_factors(dtt_ref[...], al_ref[...])
    lane_slices(s, shrink, endw_s)
    total8 = jnp.broadcast_to(grow[s.rows - 1 : s.rows, s.head_span], (8, s.heads))
    if first:
        width = halo_ref.shape[1] - bc_ref.shape[1]
        v = conv_into(bbuf[0], halo_ref[:, width:], bc_ref[...], wbc_ref[...], bbc_ref[...])
        mbc_ref[...] = (v * sigmoid(v)).astype(BF16)
    mixed_bc = mbc_ref[...].astype(F32)
    b_t = jnp.transpose(mixed_bc[:, : s.state]).astype(BF16)
    c_t = jnp.transpose(mixed_bc[:, s.state :]).astype(BF16)

    def lane_body(lane, carry):
        base = lane * s.lane_width
        for c in range(s.chunks):
            at = cols(base + c * LANES)
            wide = cols(s.base + base + c * LANES)
            v = conv_into(xbuf.at[c], halo_ref[:, wide], x_ref[:, at], wx_ref[:, wide], bx_ref[:, wide])
            mixed = (v * sigmoid(v)).astype(BF16)
            mx_ref[:, at] = mixed
            wxs_ref[:, at] = (mixed.astype(F32) * spread(s, endw_s[lane], c)).astype(BF16)
        whole = pl.ds(pl.multiple_of(base, LANES), s.lane_width)
        rows, after = slice(0, s.state), slice(s.state, s.state + 8)
        msg[lane, rows, : s.lane_width] = dot(b_t, wxs_ref[:, whole]).astype(BF16)
        msg[lane, rows, s.lane_width :] = dot(c_t, ges_ref[:, whole]).astype(BF16)
        shape = (s.heads, s.lane_width)
        pick = (iota(shape, 0) == lane * s.lane_heads + iota(shape, 1) // s.head_dim).astype(F32)
        total = dot(total8, pick, precision=EXACT)
        hi = total.astype(BF16).astype(F32)
        mid = (total - hi).astype(BF16).astype(F32)
        row = iota(total.shape, 0)
        split = jnp.where(row == 0, hi, jnp.where(row == 1, mid, jnp.where(row == 2, total - hi - mid, 0.0)))
        msg[lane, after, : s.lane_width] = split.astype(BF16)
        msg[lane, after, s.lane_width :] = split.astype(BF16)
        return carry

    lax.fori_loop(0, GROUP, lane_body, 0, unroll=True)
    for d in range(GROUP):
        outs[d][...] = msg[me ^ d]


def intra_kernel(s, first, x_ref, g_ref, mx_ref, mbc_ref, halo_ref, dtt_ref, al_ref, dsk_ref, wx_ref, bx_ref, *rest):
    if first:
        y_ref, dx_ref, slope_ref, grow_ref, shrink_ref, rs_ref, vs_ref, ds_ref, *rest = rest
    else:
        ds_in, y_ref, dx_ref, slope_ref, grow_ref, shrink_ref, rs_ref, vs_ref, dbc_ref, *rest = rest
    cum_s, ecum_s, endw_s, cumt_s, dtt_s, rs_s, vs_s, xbuf, skip_s = rest
    rows = s.rows
    _, cum_t = decay(dtt_ref[...], al_ref[...])
    lane_slices(s, jnp.transpose(cum_t), cum_s)
    grow, shrink = decay_factors(dtt_ref[...], al_ref[...])
    lane_slices(s, grow, ecum_s)
    lane_slices(s, shrink, endw_s)
    skips = jnp.broadcast_to(dsk_ref[...], (HALO, dsk_ref.shape[1]))
    lane_slices(s, skips, skip_s)
    for lane in range(GROUP):
        at = s.head0 + lane * s.lane_heads
        cumt_s[lane, 0 : s.lane_heads, :] = cum_t[at : at + s.lane_heads, :]
        dtt_s[lane, 0 : s.lane_heads, :] = dtt_ref[at : at + s.lane_heads, :]
    b, c_m = mbc_ref[:, : s.state], mbc_ref[:, s.state :]
    causal = iota((rows, rows), 0) >= iota((rows, rows), 1)
    scores = jnp.where(causal, dot(c_m, b, 1, 1), 0.0)
    lane_id = iota((rows, LANES), 1)
    masks = [((lane_id >= i * s.head_dim) & (lane_id < (i + 1) * s.head_dim)).astype(F32).astype(BF16) for i in range(s.per_chunk)]

    def lane_body(lane, d_scores):
        base = lane * s.lane_width
        row_acc = jnp.zeros((rows, LANES), F32)
        col_acc = jnp.zeros((rows, LANES), F32)
        cum_l = cum_s[lane]
        for c in range(s.chunks):
            at = cols(base + c * LANES)
            wide = cols(s.base + base + c * LANES)
            x, g = mx_ref[:, at], g_ref[:, at]
            x_st = jnp.concatenate([x * m for m in masks], axis=0)
            g_st = jnp.concatenate([g * m for m in masks], axis=0)
            d_mix = dot(g_st, x, 1, 1)
            mixes = []
            for i in range(s.per_chunk):
                h = c * s.per_chunk + i
                gap = jnp.broadcast_to(cum_l[:, h : h + 1], (rows, rows)) - cumt_s[lane, h : h + 1, :]
                e = jnp.exp(jnp.minimum(gap, 0.0)) * dtt_s[lane, h : h + 1, :]
                mixes.append((e * scores).astype(BF16))
                d_scores = d_scores + d_mix[i * rows : (i + 1) * rows, :] * e
            y = dot(jnp.concatenate(mixes, axis=1), x_st)
            dx = dot(jnp.concatenate(mixes, axis=0), g_st, 0, 0)
            xf, gf, skip = x.astype(F32), g.astype(F32), spread(s, skip_s[lane], c)[0:1, :]
            row_acc = row_acc + head_sums(s, gf * y, c)
            col_acc = col_acc + head_sums(s, xf * dx, c)
            y_ref[:, at] = (y + skip * xf).astype(BF16)
            dx_ref[:, at] = (dx + skip * gf).astype(BF16)
            grow_ref[:, at] = spread(s, ecum_s[lane], c)
            shrink_ref[:, at] = spread(s, endw_s[lane], c)
            v = conv_into(xbuf.at[c], halo_ref[:, wide], x_ref[:, at], wx_ref[:, wide], bx_ref[:, wide])
            slope_ref[:, at] = silu_slope(v)
        rs_s[lane] = row_acc
        vs_s[lane] = col_acc
        return d_scores

    start = jnp.zeros((rows, rows), F32) if first else ds_in[...]
    d_scores = lax.fori_loop(0, GROUP, lane_body, start, unroll=True)
    rs_ref[...] = lane_join(s, rs_s)
    vs_ref[...] = lane_join(s, vs_s)
    if first:
        ds_ref[...] = d_scores
    else:
        d_scores = jnp.where(causal, d_scores, 0.0).astype(BF16)
        dbc_ref[:, : s.state] = dot(d_scores, c_m, 0, 0)
        dbc_ref[:, s.state :] = dot(d_scores, b)


def place_blocks(me, srcs, buf):
    for d in range(GROUP):
        buf[me ^ d] = srcs[d][...]


def total_row(s, buf, i, at):
    return jnp.sum(buf[i, s.state : s.state + 8, at].astype(F32), axis=0, keepdims=True)


def group_sum_kernel(s, pair, at_ref, *refs):
    srcs, buf = refs[:GROUP], refs[-1]
    outs = refs[GROUP:-1]
    me, high = at_ref[0], at_ref[1]
    place_blocks(me, srcs, buf)
    for c in range(s.chunks):
        at = slice(c * LANES, (c + 1) * LANES)
        at_r = slice(s.lane_width + c * LANES, s.lane_width + (c + 1) * LANES)
        totals = [total_row(s, buf, i, at) for i in range(GROUP)]
        ahead = jnp.zeros((s.state, LANES), F32)
        back = jnp.zeros((s.state, LANES), F32)
        every = jnp.ones((1, LANES), F32)
        for i in range(GROUP):
            ahead = totals[i] * ahead + buf[i, 0 : s.state, at].astype(F32)
            r = GROUP - 1 - i
            back = totals[r] * back + buf[r, 0 : s.state, at_r].astype(F32)
            every = every * totals[i]
        if pair:
            outs[0][:, at] = jnp.where(high == 0, ahead, back).astype(BF16)
        else:
            outs[0][:, at] = ahead.astype(BF16)
            outs[1][:, at] = back.astype(BF16)
            outs[2][:, at] = jnp.broadcast_to(every, (8, LANES))


def group_scan_kernel(s, pair, at_ref, *refs):
    srcs = refs[:GROUP]
    n_in = 1 if pair else 2
    before = refs[GROUP : GROUP + n_in]
    outs = refs[GROUP + n_in : 2 * GROUP + n_in]
    buf, done = refs[2 * GROUP + n_in :]
    me, high = at_ref[0], at_ref[1]
    place_blocks(me, srcs, buf)
    for c in range(s.chunks):
        at = slice(c * LANES, (c + 1) * LANES)
        at_r = slice(s.lane_width + c * LANES, s.lane_width + (c + 1) * LANES)
        totals = [total_row(s, buf, i, at) for i in range(GROUP)]
        first = before[0][:, at].astype(F32)
        if pair:
            ahead = jnp.where(high == 1, first, 0.0)
            back = jnp.where(high == 0, first, 0.0)
        else:
            ahead, back = first, before[1][:, at].astype(F32)
        for i in range(GROUP):
            done[i, :, at] = ahead.astype(BF16)
            r = GROUP - 1 - i
            done[r, :, at_r] = back.astype(BF16)
            if i < GROUP - 1:
                ahead = totals[i] * ahead + buf[i, 0 : s.state, at].astype(F32)
                back = totals[r] * back + buf[r, 0 : s.state, at_r].astype(F32)
    for d in range(GROUP):
        outs[d][...] = done[me ^ d]


def conv_back(buf, dv, weight):
    rows, taps = dv.shape[0], weight.shape[0]
    zeros = jnp.zeros((HALO, dv.shape[1]), F32)
    buf[0:HALO, :] = zeros
    buf[HALO : HALO + rows, :] = dv
    buf[HALO + rows : 2 * HALO + rows, :] = zeros
    own = before = None
    for k in range(taps):
        w = weight[k : k + 1, :]
        first = HALO + taps - 1 - k
        part = w * buf[first : first + rows, :]
        own = part if own is None else own + part
        first = taps - 1 - k
        part = w * buf[first : first + HALO, :]
        before = part if before is None else before + part
    keep = iota(before.shape, 0) >= HALO - (taps - 1)
    return own, jnp.where(keep, before, 0.0)


def conv_weight_rows(buf, dv, taps):
    rows = dv.shape[0]
    out = []
    for k in range(taps):
        first = HALO - (taps - 1) + k
        out.append(jnp.sum(dv * buf[first : first + rows, :], axis=0, keepdims=True))
    out.append(jnp.sum(dv, axis=0, keepdims=True))
    return out


def silu_slope(v):
    sig = sigmoid(v)
    return sig * (1.0 + v * (1.0 - sig))


def pair_grads_kernel(s, lane_ref, wxs_ref, ges_ref, dbc_in, *rest):
    srcs, (dbc_ref, held) = rest[:GROUP], rest[GROUP:]
    place_blocks(lane_ref[0], srcs, held)
    d_b, d_c = dbc_in[:, : s.state], dbc_in[:, s.state :]
    for lane in range(GROUP):
        whole = slice(lane * s.lane_width, (lane + 1) * s.lane_width)
        d_c = d_c + dot(ges_ref[:, whole], held[lane, :, : s.lane_width], 1, 1)
        d_b = d_b + dot(wxs_ref[:, whole], held[lane, :, s.lane_width :], 1, 1)
    dbc_ref[:, : s.state] = d_b.astype(dbc_ref.dtype)
    dbc_ref[:, s.state :] = d_c.astype(dbc_ref.dtype)


def outputs_kernel(s, first, lane_ref, x_ref, g_ref, mx_ref, wxs_ref, ges_ref, mbc_ref, halo_ref, wx_ref, yl_ref, dxl_ref, slope_ref, grow_ref, shrink_ref, *rest):
    srcs, rest = rest[:GROUP], rest[GROUP:]
    if not first:
        rest = rest[2:]
    y_hbm, gx_hbm, gxt_ref, ho_ref, pk_ref, rs_ref, us_ref, hl_ref = rest[:8]
    held, y_s, gx_s, xbuf, dbuf, rs_s, us_s, hl_s, out_sems = rest[8:]
    place_blocks(lane_ref[0], srcs, held)

    def stores(lane):
        at = lane * s.lane_width
        here = pl.ds(pl.multiple_of(at, LANES), s.lane_width)
        there = pl.ds(pl.multiple_of(s.base + at, LANES), s.lane_width)
        return (
            pltpu.make_async_copy(y_s.at[:, here], y_hbm.at[:, there], out_sems.at[0, lane]),
            pltpu.make_async_copy(gx_s.at[:, here], gx_hbm.at[:, there], out_sems.at[1, lane]),
        )

    rows, taps = s.rows, wx_ref.shape[0]
    b, c_m = mbc_ref[:, : s.state], mbc_ref[:, s.state :]
    shape = (s.lane_width, LANES)
    pick = (iota(shape, 0) // s.head_dim == iota(shape, 1)).astype(F32).astype(BF16)
    hl_s[...] = jnp.zeros(hl_s.shape, F32)

    def lane_body(lane, carry):
        base = lane * s.lane_width
        row_acc = jnp.zeros((rows, LANES), F32)
        col_acc = jnp.zeros((rows, LANES), F32)
        links = []
        for c in range(s.chunks):
            at = cols(base + c * LANES)
            wide = cols(s.base + base + c * LANES)
            state = held[lane, :, c * LANES : (c + 1) * LANES]
            later = held[lane, :, s.lane_width + c * LANES : s.lane_width + (c + 1) * LANES]
            y = dot(c_m, state)
            row_acc = row_acc + head_sums(s, ges_ref[:, at].astype(F32) * y, c)
            y_s[:, at] = (yl_ref[:, at].astype(F32) + y * grow_ref[:, at]).astype(BF16)
            dx = dot(b, later)
            col_acc = col_acc + head_sums(s, wxs_ref[:, at].astype(F32) * dx, c)
            links.append(jnp.sum(state.astype(F32) * later.astype(F32), axis=0, keepdims=True))
            weight = wx_ref[:, wide]
            dv = (dxl_ref[:, at].astype(F32) + dx * shrink_ref[:, at]) * slope_ref[:, at]
            own, before = conv_back(dbuf.at[c], dv, weight)
            gx_s[:, at] = own.astype(BF16)
            gxt_ref[:, at] = own[rows - HALO :, :]
            ho_ref[:, at] = before.astype(BF16)
            buf = xbuf.at[c]
            buf[0:HALO, :] = halo_ref[:, wide].astype(F32)
            buf[HALO : HALO + rows, :] = x_ref[:, at].astype(F32)
            packed = conv_weight_rows(buf, dv, taps)
            packed.append(jnp.sum(g_ref[:, at].astype(F32) * mx_ref[:, at].astype(F32), axis=0, keepdims=True))
            packed.append(jnp.zeros((8 - len(packed), LANES), F32))
            pk_ref[:, at] = jnp.concatenate(packed, axis=0)
        rs_s[lane] = row_acc
        us_s[lane] = col_acc
        whole = pl.ds(pl.multiple_of(base, LANES), s.lane_width)
        skip = jnp.broadcast_to(pk_ref[taps + 1 : taps + 2, whole], (8, s.lane_width))
        link = jnp.broadcast_to(jnp.concatenate(links, axis=1), skip.shape)
        row = iota(skip.shape, 0)
        both = jnp.where(row < 2, link, skip)
        hi = both.astype(BF16).astype(F32)
        summed = dot(jnp.where(row % 2 == 0, hi, both - hi).astype(BF16), pick)
        hl_s[lane, 0:1, :] = summed[0:1, :] + summed[1:2, :]
        hl_s[lane, 1:2, :] = summed[2:3, :] + summed[3:4, :]
        for c in stores(lane):
            c.start()
        return carry

    lax.fori_loop(0, GROUP, lane_body, 0, unroll=True)
    rs_ref[...] = lane_join(s, rs_s)
    us_ref[...] = lane_join(s, us_s)
    hl_ref[...] = lane_join(s, hl_s)
    for lane in range(GROUP):
        for c in stores(lane):
            c.wait()


def tail_kernel(parts, bc_ref, halo_ref, dtt_ref, al_ref, wbc_ref, bbc_ref, dbc_ref, dbc_other, *rest):
    n = len(parts)
    groups, rest = [rest[i * 7 : (i + 1) * 7] for i in range(n)], rest[7 * n :]
    gdt_ref, pk_ref, back_ref, gbc_ref, bbuf, dbuf = rest
    taps, rows = wbc_ref.shape[0], bc_ref.shape[0]
    join = lambda i: jnp.concatenate([g[i][...] for g in groups], axis=1)
    rate, cum = decay(dtt_ref[...], al_ref[...])
    inter = jnp.transpose(join(3))
    through = jnp.transpose(join(1)) + inter
    d_cum = jnp.transpose(join(0) + join(2)) - through
    link = join(4)
    heads = rate.shape[0]
    sums = jnp.transpose(link)
    d_last = jnp.sum(inter, axis=1, keepdims=True) + jnp.exp(cum[:, rows - 1 : rows]) * sums[:, 0:1]
    d_cum = d_cum + jnp.where(iota(d_cum.shape, 1) == rows - 1, d_last, 0.0)
    d_rate = dot(d_cum, lower_ones(rows), precision=EXACT)
    step = dtt_ref[...]
    gdt_ref[...] = through / step - jnp.exp(column(al_ref[...])) * d_rate
    gal = jnp.broadcast_to(jnp.sum(rate * d_rate, axis=1, keepdims=True), (heads, LANES))
    gal = jnp.transpose(gal)[0:1, :]

    width = halo_ref.shape[1] - bc_ref.shape[1]
    v = conv_into(bbuf, halo_ref[:, width:], bc_ref[...], wbc_ref[...], bbc_ref[...])
    dv = (dbc_ref[...].astype(F32) + dbc_other[...].astype(F32)) * silu_slope(v)
    own, before = conv_back(dbuf, dv, wbc_ref[...])
    gbc_ref[...] = own
    bc_rows = conv_weight_rows(bbuf, dv, taps)
    pk_ref[...] = jnp.zeros(pk_ref.shape, pk_ref.dtype)
    for s, g in zip(parts, groups):
        pk_ref[0 : taps + 1, s.span] = g[5][0 : taps + 1, :].astype(BF16)
        back_ref[:, s.span] = g[6][...]
    back_ref[:, width:] = before.astype(BF16)
    row = taps + 1
    pk_ref[row : row + 1, 0:heads] = gal.astype(BF16)
    pk_ref[row : row + 1, LANES : LANES + heads] = link[1:2, :].astype(BF16)
    for k, r in enumerate(bc_rows):
        at = 2 * LANES + k * r.shape[1]
        pk_ref[row : row + 1, at : at + r.shape[1]] = r.astype(BF16)


def finish_kernel(parts, taps, heads, gx_in, pk_ref, other_ref, back_ref, gbc_ref, *rest):
    n = len(parts)
    tails, rest = rest[:n], rest[n:]
    gx_hbm, grad_bc, gwx_ref, gwbc_ref, gbx_ref, gal_ref, gsk_ref, gbbc_ref, gxt, sem = rest
    rows = gbc_ref.shape[0]
    width = gxt.shape[1]
    for s, t in zip(parts, tails):
        gxt[:, s.span] = (t[...] + back_ref[:, s.span].astype(F32)).astype(BF16)
    store = pltpu.make_async_copy(gxt, gx_hbm.at[rows - HALO : rows, :], sem)
    store.start()
    grad_bc[...] = gbc_ref[...].astype(BF16)
    tail = gbc_ref[rows - HALO : rows, :] + back_ref[:, width:].astype(F32)
    grad_bc[rows - HALO : rows, :] = tail.astype(BF16)
    total = pk_ref[...].astype(F32) + other_ref[...].astype(F32)
    gwx_ref[...] = total[0:taps, :]
    bc_width = gbc_ref.shape[1]
    row = total[taps + 1 : taps + 2, :]
    for k in range(taps):
        at = 2 * LANES + k * bc_width
        gwbc_ref[k : k + 1, :] = row[:, at : at + bc_width]
    gbx_ref[...] = total[taps]
    row = total[taps + 1]
    gal_ref[...] = row[0:heads]
    gsk_ref[...] = row[LANES : LANES + heads]
    at = 2 * LANES + taps * bc_width
    gbbc_ref[...] = row[at : at + bc_width]
    store.wait()


VMEM = pl.BlockSpec(memory_space=pltpu.VMEM)
SMEM = pl.BlockSpec(memory_space=pltpu.SMEM)
ANY = pl.BlockSpec(memory_space=pl.ANY)
HBM = pl.BlockSpec(memory_space=pltpu.HBM)


def call(kernel, name, args, in_specs, outs, out_specs, scratch, flops=0, after=(), aliases=None):
    n, extra = len(args), len(after)

    def body(*refs):
        kernel(*refs[:n], *refs[n + extra :])

    moved = sum(a.size * a.dtype.itemsize for a in (*args, *outs))
    return pl.pallas_call(
        body,
        name=name,
        out_shape=tuple(outs),
        in_specs=list(in_specs) + [ANY] * extra,
        out_specs=tuple(out_specs),
        scratch_shapes=scratch,
        input_output_aliases=aliases or {},
        compiler_params=pltpu.CompilerParams(vmem_limit_bytes=12 << 20),
        cost_estimate=pl.CostEstimate(flops=flops, bytes_accessed=moved, transcendentals=0),
    )(*args, *after)


def shift(value, count, steps):
    pairs = [(i, i + steps) for i in range(count) if 0 <= i + steps < count]
    return lax.ppermute(value, "ctx", pairs)


def swap(value, count, mask):
    return lax.ppermute(value, "ctx", [(i, i ^ mask) for i in range(count)])


def group_scan(ahead, back, every, count):
    found = []
    for sign, value in ((1, ahead), (-1, back)):
        total = shift(every, count, sign * GROUP)
        value = shift(value, count, sign * GROUP).astype(F32)
        step = GROUP
        while step < count:
            value = value + total[0:1] * shift(value.astype(BF16), count, sign * step).astype(F32)
            total = total * shift(total, count, sign * step)
            step *= 2
        found.append(value.astype(BF16))
    return found


def local(n_ctx, x_in, bc_in, step_dt, a_log, d_skip, conv_wx, conv_bx, conv_wbc, conv_bbc, grad_out):
    rows, width = x_in.shape
    heads, state = step_dt.shape[1], bc_in.shape[1] // 2
    head_dim = width // heads
    taps = conv_wx.shape[0]
    n_chunks = width // (GROUP * LANES)
    cut = (n_chunks + 1) // 2
    parts = [Part(rows, state, head_dim, 0, cut), Part(rows, state, head_dim, cut * GROUP * LANES, n_chunks - cut)]
    pair = n_ctx == 2 * GROUP
    index = lax.axis_index("ctx")
    place = jnp.stack([index % GROUP, index // GROUP]).astype(jnp.int32)
    sds = jax.ShapeDtypeStruct
    vm = pltpu.VMEM

    halo = shift(jnp.concatenate([x_in[-HALO:], bc_in[-HALO:]], axis=1), n_ctx, 1)
    bx, bbc = conv_bx[None, :], conv_bbc[None, :]
    msg_rows = state + 8
    per_head = vm((GROUP, rows, LANES), F32)
    bc_shape = (rows, 2 * state)

    def factors():
        args = [pltpu.with_memory_space_constraint(v, pltpu.HBM) for v in (x_in, grad_out, step_dt.T, a_log[None, :])]
        outs = []
        for s in parts:
            outs += [sds((rows, s.width), BF16)] * 3
        outs += [sds((heads, rows), F32), sds((1, heads), F32)]
        found = call(
            functools.partial(factors_kernel, parts),
            "factors",
            args,
            [HBM] * 4,
            outs,
            [VMEM] * len(outs),
            [per_head, pltpu.SemaphoreType.DMA((2 * len(parts) + 2,))],
        )
        return found[:3], found[3:6], *found[6:]

    def states(s, first, fac, extra, after=()):
        x, _, ges = fac
        args = (place, x, ges, step_t, al, halo, conv_wx, bx, *extra)
        wide = sds((rows, s.width), BF16)
        msgs = [sds((msg_rows, 2 * s.lane_width), BF16)] * GROUP
        return call(
            functools.partial(states_kernel, s, first),
            "states",
            args,
            [SMEM] + [VMEM] * (len(args) - 1),
            ([sds(bc_shape, BF16)] if first else []) + [wide] * 2 + msgs,
            [VMEM] * ((3 if first else 2) + GROUP),
            [vm((GROUP, msg_rows, 2 * s.lane_width), BF16), per_head, vm((s.chunks, rows + HALO, LANES), F32)]
            + ([vm((rows + HALO, 2 * state), F32)] if first else []),
            4 * rows * s.width * state,
            after,
        )

    def exchange(messages):
        return [messages[0]] + [swap(messages[d], n_ctx, d) for d in range(1, GROUP)]

    def intra(s, first, fac, mx, d_scores, after=()):
        x, g = fac[:2]
        args = (x, g, mx, mbc, halo, step_t, al, skip, conv_wx, bx) + (() if first else (d_scores,))
        per_row = vm((GROUP, 16, rows), F32)
        return call(
            functools.partial(intra_kernel, s, first),
            "intra",
            args,
            [VMEM] * len(args),
            [sds((rows, s.width), BF16)] * 2
            + [sds((rows, s.width), F32)] * 3
            + [sds((rows, s.heads), F32)] * 2
            + [sds((rows, rows) if first else bc_shape, F32)],
            [VMEM] * 8,
            [per_head, per_head, per_head, per_row, per_row, per_head, per_head, vm((s.chunks, rows + HALO, LANES), F32), vm((GROUP, HALO, LANES), F32)],
            12 * rows * s.width * rows,
            after,
        )

    def sums(s, blocks, after=()):
        shape = (state, s.lane_width)
        outs = [sds(shape, BF16)] if pair else [sds(shape, BF16)] * 2 + [sds((8, s.lane_width), F32)]
        summed = call(
            functools.partial(group_sum_kernel, s, pair),
            "group_sum",
            (place, *blocks),
            [SMEM] + [VMEM] * GROUP,
            outs,
            [VMEM] * len(outs),
            [vm((GROUP, msg_rows, 2 * s.lane_width), BF16)],
            state * s.width,
            after,
        )
        return [swap(summed[0], n_ctx, GROUP)] if pair else group_scan(*summed, n_ctx)

    def scan(s, blocks, before, after=()):
        return call(
            functools.partial(group_scan_kernel, s, pair),
            "group_scan",
            (place, *blocks, *before),
            [SMEM] + [VMEM] * GROUP + [VMEM] * len(before),
            [sds((state, 2 * s.lane_width), BF16)] * GROUP,
            [VMEM] * GROUP,
            [vm((GROUP, msg_rows, 2 * s.lane_width), BF16), vm((GROUP, state, 2 * s.lane_width), BF16)],
            state * s.width,
            after,
        )

    def pair_grads(s, wxs, ges, dbc, held, dtype, after=()):
        return call(
            functools.partial(pair_grads_kernel, s),
            "pair_grads",
            (place, wxs, ges, dbc, *held),
            [SMEM] + [VMEM] * 3 + [VMEM] * GROUP,
            [sds(bc_shape, dtype)],
            [VMEM],
            [vm((GROUP, state, 2 * s.lane_width), BF16)],
            4 * rows * s.width * state,
            after,
        )[0]

    def outputs(s, first, fac, mx, wxs, inner, held, whole, after=()):
        x, g, ges = fac[:3]
        args = (place, x, g, mx, wxs, ges, mbc, halo, conv_wx, *inner[:5], *held, *whole)
        return call(
            functools.partial(outputs_kernel, s, first),
            "outputs",
            args,
            [SMEM] + [VMEM] * 13 + [VMEM] * GROUP + [HBM] * len(whole),
            [sds((rows, width), BF16)] * 2
            + [sds((HALO, s.width), F32), sds((HALO, s.width), BF16), sds((8, s.width), F32)]
            + [sds((rows, s.heads), F32)] * 2
            + [sds((8, s.heads), F32)],
            [HBM, HBM] + [VMEM] * 6,
            [
                vm((GROUP, state, 2 * s.lane_width), BF16),
                vm((rows, s.width), BF16),
                vm((rows, s.width), BF16),
                vm((s.chunks, rows + HALO, LANES), F32),
                vm((s.chunks, rows + 2 * HALO, LANES), F32),
                per_head,
                per_head,
                vm((GROUP, 8, LANES), F32),
                pltpu.SemaphoreType.DMA((2, GROUP)),
            ],
            4 * rows * s.width * state,
            after,
            {} if first else {14 + GROUP: 0, 15 + GROUP: 1},
        )

    a, b = parts
    skip = d_skip[None, :]
    fac_a, fac_b, step_t, al = factors()
    mbc, mx_a, wxs_a, *msgs = states(a, True, fac_a, (bc_in, conv_wbc, bbc))
    blocks_a = exchange(msgs)
    mx_b, wxs_b, *msgs = states(b, False, fac_b, (mbc,))
    blocks_b = exchange(msgs)
    inner_a = intra(a, True, fac_a, mx_a, None, (msgs[0],))
    before_a = sums(a, blocks_a, (inner_a[-1],))
    before_b = sums(b, blocks_b)
    inner_b = intra(b, False, fac_b, mx_b, inner_a[-1])
    held_a = exchange(scan(a, blocks_a, before_a, (inner_b[-1],)))
    held_b = exchange(scan(b, blocks_b, before_b))
    dbc = pair_grads(a, wxs_a, fac_a[2], inner_b[-1], held_a, F32)
    out_a = outputs(a, True, fac_a, mx_a, wxs_a, inner_a, held_a, ())
    dbc = pair_grads(b, wxs_b, fac_b[2], dbc, held_b, BF16, (out_a[-1],))
    n_head = lax.axis_size("head")
    if n_head == 2:
        other = lax.ppermute(dbc, "head", [(0, 1), (1, 0)])
    else:
        other = (lax.psum(dbc.astype(F32), "head") - dbc.astype(F32)).astype(BF16)
    out_b = outputs(b, False, fac_b, mx_b, wxs_b, inner_b, held_b, out_a[:2])
    y, gx = out_b[:2]

    args = [bc_in, halo, step_t, al, conv_wbc, bbc, dbc, other]
    for inner, out in ((inner_a, out_a), (inner_b, out_b)):
        args += [inner[5], inner[6], out[5], out[6], out[7], out[4], out[3]]
    gdt_t, packed, back, gbc = call(
        functools.partial(tail_kernel, parts),
        "tail",
        tuple(args),
        [VMEM] * len(args),
        [sds((heads, rows), F32), sds((8, width), BF16), sds((HALO, width + 2 * state), BF16), sds(bc_shape, F32)],
        [VMEM] * 4,
        [vm((rows + HALO, 2 * state), F32), vm((rows + 2 * HALO, 2 * state), F32)],
    )
    back = shift(back, n_ctx, -1)
    step = 1
    while 2 * step < n_ctx:
        packed = packed + swap(packed, n_ctx, step)
        step *= 2
    last = swap(packed, n_ctx, step)
    args = (gx, packed, last, back, gbc, out_a[2], out_b[2])
    gx, grad_bc, gwx, gwbc, gbx, gal, gskip, gbbc = call(
        functools.partial(finish_kernel, parts, taps, heads),
        "finish",
        args,
        [HBM] + [VMEM] * (len(args) - 1),
        [sds((rows, width), BF16), sds(bc_shape, BF16), sds((taps, width), F32), sds((taps, 2 * state), F32)]
        + [sds((n,), F32) for n in (width, heads, heads, 2 * state)],
        [HBM] + [VMEM] * 7,
        [vm((HALO, width), BF16), pltpu.SemaphoreType.DMA],
        aliases={0: 0},
    )
    return y, gx, grad_bc, gdt_t.T, gal, gskip, gwx, gbx, gwbc, gbbc


def solution(mesh):
    rows, both = P(("groups", "ctx"), "head"), P(("groups", "head"))
    return jax.shard_map(
        functools.partial(local, mesh.shape["ctx"]),
        mesh=mesh,
        in_specs=(rows, P(("groups", "ctx"), None), rows, P("head"), P("head"), P(None, "head"), P("head"), P(), P(), rows),
        out_specs=(rows, rows, P(("groups", "ctx"), None), rows, both, both, P("groups", "head"), both, P("groups", None), P("groups")),
        check_vma=False,
    )
```

```python
import functools

import jax
import jax.numpy as jnp
from jax import lax
from jax.experimental import pallas as pl
from jax.experimental.pallas import tpu as pltpu
from jax.sharding import PartitionSpec as P

F32, BF16 = jnp.float32, jnp.bfloat16
EXACT = lax.Precision.HIGHEST
LANES = 128
HALO = 8
GROUP = 4


def dot(a, b, ca=1, cb=0, precision=None):
    dims = (((ca,), (cb,)), ((), ()))
    return lax.dot_general(a, b, dims, preferred_element_type=F32, precision=precision)


def iota(shape, dim):
    return lax.broadcasted_iota(jnp.int32, shape, dim)


def lower_ones(size):
    return (iota((size, size), 0) >= iota((size, size), 1)).astype(F32)


def upper_ones(size):
    return (iota((size, size), 0) <= iota((size, size), 1)).astype(F32)


def sigmoid(v):
    return 1.0 / (1.0 + jnp.exp(-v))


def cols(start):
    return pl.ds(pl.multiple_of(start, LANES), LANES)


class Part:
    def __init__(self, rows, state, head_dim, base, chunks):
        self.rows, self.state, self.head_dim, self.base, self.chunks = rows, state, head_dim, base, chunks
        self.lane_width = chunks * LANES
        self.width = GROUP * self.lane_width
        self.per_chunk = LANES // head_dim
        self.lane_heads = chunks * self.per_chunk
        self.heads = GROUP * self.lane_heads
        self.head0 = base // head_dim
        self.span = slice(base, base + self.width)
        self.head_span = slice(self.head0, self.head0 + self.heads)


def lane_slices(s, value, scratch):
    for lane in range(GROUP):
        at = s.head0 + lane * s.lane_heads
        scratch[lane, :, 0 : s.lane_heads] = value[:, at : at + s.lane_heads]


def lane_join(s, scratch):
    return jnp.concatenate([scratch[lane][:, 0 : s.lane_heads] for lane in range(GROUP)], axis=1)


def spread(s, value, chunk):
    rows = value.shape[0]
    lane = iota((rows, LANES), 1)
    out = None
    for i in range(s.per_chunk):
        h = chunk * s.per_chunk + i
        col = jnp.broadcast_to(value[:, h : h + 1], (rows, LANES))
        out = col if out is None else jnp.where(lane >= i * s.head_dim, col, out)
    return out


def head_sums(s, value, chunk):
    r, c = iota((LANES, LANES), 0), iota((LANES, LANES), 1)
    one = (c == chunk * s.per_chunk + r // s.head_dim).astype(F32).astype(BF16)
    hi = value.astype(BF16)
    lo = (value - hi.astype(F32)).astype(BF16)
    return dot(jnp.concatenate([hi, lo], axis=1), jnp.concatenate([one, one], axis=0))


def column(row):
    return jnp.transpose(jnp.broadcast_to(row, (8, row.shape[1])))[:, 0:1]


def decay(step_t, alog):
    rate = -step_t * jnp.exp(column(alog))
    return rate, dot(rate, upper_ones(step_t.shape[1]), precision=EXACT)


def decay_factors(step_t, alog):
    _, cum = decay(step_t, alog)
    rows = step_t.shape[1]
    last = cum[:, rows - 1 : rows]
    return jnp.transpose(jnp.exp(cum)), jnp.transpose(jnp.exp(last - cum) * step_t)


def conv_into(buf, halo, x, weight, bias):
    rows = x.shape[0]
    buf[0:HALO, :] = halo.astype(F32)
    buf[HALO : HALO + rows, :] = x.astype(F32)
    taps = weight.shape[0]
    total = jnp.broadcast_to(bias, x.shape)
    for k in range(taps):
        first = HALO - (taps - 1) + k
        total = total + weight[k : k + 1, :] * buf[first : first + rows, :]
    return total


def factors_kernel(parts, n_small, x_hbm, g_hbm, *refs):
    n = len(parts)
    given, refs = refs[:n_small], refs[n_small:]
    outs, refs = [refs[3 * i : 3 * i + 3] for i in range(n)], refs[3 * n :]
    taken, refs = refs[:n_small], refs[n_small:]
    ecum_s, sems, *flat = refs
    targets = [flat.pop(0) if len(ref.shape) == 1 else to for ref, to in zip(given, taken)]
    small = [pltpu.make_async_copy(ref, to, sems.at[2 * n + k]) for k, (ref, to) in enumerate(zip(given, targets))]
    for c in small:
        c.start()
    loads = []
    for i, (s, out) in enumerate(zip(parts, outs)):
        loads.append(
            [
                pltpu.make_async_copy(g_hbm.at[:, s.span], out[1], sems.at[2 * i]),
                pltpu.make_async_copy(x_hbm.at[:, s.span], out[0], sems.at[2 * i + 1]),
            ]
        )
        for c in loads[-1]:
            c.start()
    for c in small:
        c.wait()
    for ref, at, to in zip(given, targets, taken):
        if len(ref.shape) == 1:
            to[...] = at[...][None, :]
    grow, _ = decay_factors(taken[0][...], taken[1][...])
    for s, out, load in zip(parts, outs, loads):
        _, g_ref, ges_ref = out
        lane_slices(s, grow, ecum_s)

        load[0].wait()

        def scale_body(lane, carry):
            for c in range(s.chunks):
                at = cols(lane * s.lane_width + c * LANES)
                ges_ref[:, at] = (g_ref[:, at].astype(F32) * spread(s, ecum_s[lane], c)).astype(BF16)
            return carry

        lax.fori_loop(0, GROUP, scale_body, 0, unroll=True)
    for load in loads:
        load[1].wait()


def states_kernel(s, first, lane_ref, x_ref, ges_ref, dtt_ref, al_ref, halo_ref, wx_ref, bx_ref, *rest):
    if first:
        bc_ref, wbc_ref, bbc_ref, mbc_ref, *rest = rest
    else:
        mbc_ref, *rest = rest
    mx_ref, wxs_ref = rest[:2]
    outs = rest[2 : 2 + GROUP]
    msg, endw_s, xbuf, *bbuf = rest[2 + GROUP :]
    me = lane_ref[0]
    grow, shrink = decay_factors(dtt_ref[...], al_ref[...])
    lane_slices(s, shrink, endw_s)
    total8 = jnp.broadcast_to(grow[s.rows - 1 : s.rows, s.head_span], (8, s.heads))
    if first:
        width = halo_ref.shape[1] - bc_ref.shape[1]
        v = conv_into(bbuf[0], halo_ref[:, width:], bc_ref[...], wbc_ref[...], bbc_ref[...])
        mbc_ref[...] = (v * sigmoid(v)).astype(BF16)
    mixed_bc = mbc_ref[...].astype(F32)
    b_t = jnp.transpose(mixed_bc[:, : s.state]).astype(BF16)
    c_t = jnp.transpose(mixed_bc[:, s.state :]).astype(BF16)

    def lane_body(lane, carry):
        base = lane * s.lane_width
        for c in range(s.chunks):
            at = cols(base + c * LANES)
            wide = cols(s.base + base + c * LANES)
            v = conv_into(xbuf.at[c], halo_ref[:, wide], x_ref[:, at], wx_ref[:, wide], bx_ref[:, wide])
            mixed = (v * sigmoid(v)).astype(BF16)
            mx_ref[:, at] = mixed
            wxs_ref[:, at] = (mixed.astype(F32) * spread(s, endw_s[lane], c)).astype(BF16)
        whole = pl.ds(pl.multiple_of(base, LANES), s.lane_width)
        rows, after = slice(0, s.state), slice(s.state, s.state + 8)
        msg[lane, rows, : s.lane_width] = dot(b_t, wxs_ref[:, whole]).astype(BF16)
        msg[lane, rows, s.lane_width :] = dot(c_t, ges_ref[:, whole]).astype(BF16)
        shape = (s.heads, s.lane_width)
        pick = (iota(shape, 0) == lane * s.lane_heads + iota(shape, 1) // s.head_dim).astype(F32)
        total = dot(total8, pick, precision=EXACT)
        hi = total.astype(BF16).astype(F32)
        mid = (total - hi).astype(BF16).astype(F32)
        row = iota(total.shape, 0)
        split = jnp.where(row == 0, hi, jnp.where(row == 1, mid, jnp.where(row == 2, total - hi - mid, 0.0)))
        msg[lane, after, : s.lane_width] = split.astype(BF16)
        msg[lane, after, s.lane_width :] = split.astype(BF16)
        return carry

    lax.fori_loop(0, GROUP, lane_body, 0, unroll=True)
    for d in range(GROUP):
        outs[d][...] = msg[me ^ d]


def intra_kernel(s, first, x_ref, g_ref, mx_ref, mbc_ref, halo_ref, dtt_ref, al_ref, dsk_ref, wx_ref, bx_ref, *rest):
    if first:
        y_ref, dx_ref, slope_ref, grow_ref, shrink_ref, rs_ref, vs_ref, ds_ref, *rest = rest
    else:
        ds_in, y_ref, dx_ref, slope_ref, grow_ref, shrink_ref, rs_ref, vs_ref, dbc_ref, *rest = rest
    cum_s, ecum_s, endw_s, cumt_s, dtt_s, rs_s, vs_s, xbuf, skip_s = rest
    rows = s.rows
    _, cum_t = decay(dtt_ref[...], al_ref[...])
    lane_slices(s, jnp.transpose(cum_t), cum_s)
    grow, shrink = decay_factors(dtt_ref[...], al_ref[...])
    lane_slices(s, grow, ecum_s)
    lane_slices(s, shrink, endw_s)
    skips = jnp.broadcast_to(dsk_ref[...], (HALO, dsk_ref.shape[1]))
    lane_slices(s, skips, skip_s)
    for lane in range(GROUP):
        at = s.head0 + lane * s.lane_heads
        cumt_s[lane, 0 : s.lane_heads, :] = cum_t[at : at + s.lane_heads, :]
        dtt_s[lane, 0 : s.lane_heads, :] = dtt_ref[at : at + s.lane_heads, :]
    b, c_m = mbc_ref[:, : s.state], mbc_ref[:, s.state :]
    causal = iota((rows, rows), 0) >= iota((rows, rows), 1)
    scores = jnp.where(causal, dot(c_m, b, 1, 1), 0.0)
    lane_id = iota((rows, LANES), 1)
    masks = [((lane_id >= i * s.head_dim) & (lane_id < (i + 1) * s.head_dim)).astype(F32).astype(BF16) for i in range(s.per_chunk)]

    def lane_body(lane, d_scores):
        base = lane * s.lane_width
        row_acc = jnp.zeros((rows, LANES), F32)
        col_acc = jnp.zeros((rows, LANES), F32)
        cum_l = cum_s[lane]
        for c in range(s.chunks):
            at = cols(base + c * LANES)
            wide = cols(s.base + base + c * LANES)
            x, g = mx_ref[:, at], g_ref[:, at]
            x_st = jnp.concatenate([x * m for m in masks], axis=0)
            g_st = jnp.concatenate([g * m for m in masks], axis=0)
            d_mix = dot(g_st, x, 1, 1)
            mixes = []
            for i in range(s.per_chunk):
                h = c * s.per_chunk + i
                gap = jnp.broadcast_to(cum_l[:, h : h + 1], (rows, rows)) - cumt_s[lane, h : h + 1, :]
                e = jnp.exp(jnp.minimum(gap, 0.0)) * dtt_s[lane, h : h + 1, :]
                mixes.append((e * scores).astype(BF16))
                d_scores = d_scores + d_mix[i * rows : (i + 1) * rows, :] * e
            y = dot(jnp.concatenate(mixes, axis=1), x_st)
            dx = dot(jnp.concatenate(mixes, axis=0), g_st, 0, 0)
            xf, gf, skip = x.astype(F32), g.astype(F32), spread(s, skip_s[lane], c)[0:1, :]
            row_acc = row_acc + head_sums(s, gf * y, c)
            col_acc = col_acc + head_sums(s, xf * dx, c)
            y_ref[:, at] = (y + skip * xf).astype(BF16)
            dx_ref[:, at] = (dx + skip * gf).astype(BF16)
            grow_ref[:, at] = spread(s, ecum_s[lane], c)
            shrink_ref[:, at] = spread(s, endw_s[lane], c)
            v = conv_into(xbuf.at[c], halo_ref[:, wide], x_ref[:, at], wx_ref[:, wide], bx_ref[:, wide])
            slope_ref[:, at] = silu_slope(v)
        rs_s[lane] = row_acc
        vs_s[lane] = col_acc
        return d_scores

    start = jnp.zeros((rows, rows), F32) if first else ds_in[...]
    d_scores = lax.fori_loop(0, GROUP, lane_body, start, unroll=True)
    rs_ref[...] = lane_join(s, rs_s)
    vs_ref[...] = lane_join(s, vs_s)
    if first:
        ds_ref[...] = d_scores
    else:
        d_scores = jnp.where(causal, d_scores, 0.0).astype(BF16)
        dbc_ref[:, : s.state] = dot(d_scores, c_m, 0, 0)
        dbc_ref[:, s.state :] = dot(d_scores, b)


def place_blocks(me, srcs, buf):
    for d in range(GROUP):
        buf[me ^ d] = srcs[d][...]


def total_row(s, buf, i, at):
    return jnp.sum(buf[i, s.state : s.state + 8, at].astype(F32), axis=0, keepdims=True)


def group_sum_kernel(s, pair, at_ref, *refs):
    srcs, buf = refs[:GROUP], refs[-1]
    outs = refs[GROUP:-1]
    me, high = at_ref[0], at_ref[1]
    place_blocks(me, srcs, buf)
    for c in range(s.chunks):
        at = slice(c * LANES, (c + 1) * LANES)
        at_r = slice(s.lane_width + c * LANES, s.lane_width + (c + 1) * LANES)
        totals = [total_row(s, buf, i, at) for i in range(GROUP)]
        ahead = jnp.zeros((s.state, LANES), F32)
        back = jnp.zeros((s.state, LANES), F32)
        every = jnp.ones((1, LANES), F32)
        for i in range(GROUP):
            ahead = totals[i] * ahead + buf[i, 0 : s.state, at].astype(F32)
            r = GROUP - 1 - i
            back = totals[r] * back + buf[r, 0 : s.state, at_r].astype(F32)
            every = every * totals[i]
        if pair:
            outs[0][:, at] = jnp.where(high == 0, ahead, back).astype(BF16)
        else:
            outs[0][:, at] = ahead.astype(BF16)
            outs[1][:, at] = back.astype(BF16)
            outs[2][:, at] = jnp.broadcast_to(every, (8, LANES))


def group_scan_kernel(s, pair, at_ref, *refs):
    srcs = refs[:GROUP]
    n_in = 1 if pair else 2
    before = refs[GROUP : GROUP + n_in]
    outs = refs[GROUP + n_in : 2 * GROUP + n_in]
    buf, done = refs[2 * GROUP + n_in :]
    me, high = at_ref[0], at_ref[1]
    place_blocks(me, srcs, buf)
    for c in range(s.chunks):
        at = slice(c * LANES, (c + 1) * LANES)
        at_r = slice(s.lane_width + c * LANES, s.lane_width + (c + 1) * LANES)
        totals = [total_row(s, buf, i, at) for i in range(GROUP)]
        first = before[0][:, at].astype(F32)
        if pair:
            ahead = jnp.where(high == 1, first, 0.0)
            back = jnp.where(high == 0, first, 0.0)
        else:
            ahead, back = first, before[1][:, at].astype(F32)
        for i in range(GROUP):
            done[i, :, at] = ahead.astype(BF16)
            r = GROUP - 1 - i
            done[r, :, at_r] = back.astype(BF16)
            if i < GROUP - 1:
                ahead = totals[i] * ahead + buf[i, 0 : s.state, at].astype(F32)
                back = totals[r] * back + buf[r, 0 : s.state, at_r].astype(F32)
    for d in range(GROUP):
        outs[d][...] = done[me ^ d]


def conv_back(buf, dv, weight):
    rows, taps = dv.shape[0], weight.shape[0]
    zeros = jnp.zeros((HALO, dv.shape[1]), F32)
    buf[0:HALO, :] = zeros
    buf[HALO : HALO + rows, :] = dv
    buf[HALO + rows : 2 * HALO + rows, :] = zeros
    own = before = None
    for k in range(taps):
        w = weight[k : k + 1, :]
        first = HALO + taps - 1 - k
        part = w * buf[first : first + rows, :]
        own = part if own is None else own + part
        first = taps - 1 - k
        part = w * buf[first : first + HALO, :]
        before = part if before is None else before + part
    keep = iota(before.shape, 0) >= HALO - (taps - 1)
    return own, jnp.where(keep, before, 0.0)


def rows_before(buf, dv, weight):
    taps = weight.shape[0]
    buf[0:HALO, :] = jnp.zeros((HALO, dv.shape[1]), F32)
    buf[HALO : 2 * HALO, :] = dv[0:HALO, :]
    before = None
    for k in range(taps):
        first = taps - 1 - k
        part = weight[k : k + 1, :] * buf[first : first + HALO, :]
        before = part if before is None else before + part
    return jnp.where(iota(before.shape, 0) >= HALO - (taps - 1), before, 0.0)


def rows_own(buf, dv, weight):
    rows, taps = dv.shape[0], weight.shape[0]
    buf[0:rows, :] = dv
    buf[rows : rows + HALO, :] = jnp.zeros((HALO, dv.shape[1]), F32)
    own = None
    for k in range(taps):
        first = taps - 1 - k
        part = weight[k : k + 1, :] * buf[first : first + rows, :]
        own = part if own is None else own + part
    return own


def conv_weight_rows(buf, dv, taps):
    rows = dv.shape[0]
    out = []
    for k in range(taps):
        first = HALO - (taps - 1) + k
        out.append(jnp.sum(dv * buf[first : first + rows, :], axis=0, keepdims=True))
    out.append(jnp.sum(dv, axis=0, keepdims=True))
    return out


def silu_slope(v):
    sig = sigmoid(v)
    return sig * (1.0 + v * (1.0 - sig))


def pair_grads_kernel(s, lane_ref, wxs_ref, ges_ref, dbc_in, *rest):
    srcs, (dbc_ref, held) = rest[:GROUP], rest[GROUP:]
    place_blocks(lane_ref[0], srcs, held)
    d_b, d_c = dbc_in[:, : s.state], dbc_in[:, s.state :]
    for lane in range(GROUP):
        whole = slice(lane * s.lane_width, (lane + 1) * s.lane_width)
        d_c = d_c + dot(ges_ref[:, whole], held[lane, :, : s.lane_width], 1, 1)
        d_b = d_b + dot(wxs_ref[:, whole], held[lane, :, s.lane_width :], 1, 1)
    dbc_ref[:, : s.state] = d_b.astype(dbc_ref.dtype)
    dbc_ref[:, s.state :] = d_c.astype(dbc_ref.dtype)


def outputs_kernel(s, first, lane_ref, x_ref, g_ref, mx_ref, wxs_ref, ges_ref, mbc_ref, halo_ref, wx_ref, yl_ref, dxl_ref, slope_ref, grow_ref, shrink_ref, *rest):
    srcs, rest = rest[:GROUP], rest[GROUP:]
    if first:
        y_hbm, gx_hbm, gxt_ref, *rest = rest
    else:
        y_s, dv_ref, *rest = rest
    ho_ref, pk_ref, rs_ref, us_ref, hl_ref, *rest = rest
    held, xbuf, dbuf, rs_s, us_s, hl_s, *rest = rest
    if first:
        y_s, gx_s, out_sems = rest
    place_blocks(lane_ref[0], srcs, held)

    def stores(lane):
        at = lane * s.lane_width
        here = pl.ds(pl.multiple_of(at, LANES), s.lane_width)
        there = pl.ds(pl.multiple_of(s.base + at, LANES), s.lane_width)
        return (
            pltpu.make_async_copy(y_s.at[:, here], y_hbm.at[:, there], out_sems.at[0, lane]),
            pltpu.make_async_copy(gx_s.at[:, here], gx_hbm.at[:, there], out_sems.at[1, lane]),
        )

    rows, taps = s.rows, wx_ref.shape[0]
    b, c_m = mbc_ref[:, : s.state], mbc_ref[:, s.state :]
    shape = (s.lane_width, LANES)
    pick = (iota(shape, 0) // s.head_dim == iota(shape, 1)).astype(F32).astype(BF16)
    hl_s[...] = jnp.zeros(hl_s.shape, F32)

    def lane_body(lane, carry):
        base = lane * s.lane_width
        row_acc = jnp.zeros((rows, LANES), F32)
        col_acc = jnp.zeros((rows, LANES), F32)
        links = []
        for c in range(s.chunks):
            at = cols(base + c * LANES)
            wide = cols(s.base + base + c * LANES)
            state = held[lane, :, c * LANES : (c + 1) * LANES]
            later = held[lane, :, s.lane_width + c * LANES : s.lane_width + (c + 1) * LANES]
            y = dot(c_m, state)
            row_acc = row_acc + head_sums(s, ges_ref[:, at].astype(F32) * y, c)
            y_s[:, at] = (yl_ref[:, at].astype(F32) + y * grow_ref[:, at]).astype(BF16)
            dx = dot(b, later)
            col_acc = col_acc + head_sums(s, wxs_ref[:, at].astype(F32) * dx, c)
            links.append(jnp.sum(state.astype(F32) * later.astype(F32), axis=0, keepdims=True))
            weight = wx_ref[:, wide]
            dv = (dxl_ref[:, at].astype(F32) + dx * shrink_ref[:, at]) * slope_ref[:, at]
            if first:
                own, before = conv_back(dbuf.at[c], dv, weight)
                gx_s[:, at] = own.astype(BF16)
                gxt_ref[:, at] = own[rows - HALO :, :]
            else:
                before = rows_before(dbuf.at[c], dv, weight)
                dv_ref[:, at] = dv
            ho_ref[:, at] = before.astype(BF16)
            buf = xbuf.at[c]
            buf[0:HALO, :] = halo_ref[:, wide].astype(F32)
            buf[HALO : HALO + rows, :] = x_ref[:, at].astype(F32)
            packed = conv_weight_rows(buf, dv, taps)
            packed.append(jnp.sum(g_ref[:, at].astype(F32) * mx_ref[:, at].astype(F32), axis=0, keepdims=True))
            packed.append(jnp.zeros((8 - len(packed), LANES), F32))
            pk_ref[:, at] = jnp.concatenate(packed, axis=0)
        rs_s[lane] = row_acc
        us_s[lane] = col_acc
        whole = pl.ds(pl.multiple_of(base, LANES), s.lane_width)
        skip = jnp.broadcast_to(pk_ref[taps + 1 : taps + 2, whole], (8, s.lane_width))
        link = jnp.broadcast_to(jnp.concatenate(links, axis=1), skip.shape)
        row = iota(skip.shape, 0)
        both = jnp.where(row < 2, link, skip)
        hi = both.astype(BF16).astype(F32)
        summed = dot(jnp.where(row % 2 == 0, hi, both - hi).astype(BF16), pick)
        hl_s[lane, 0:1, :] = summed[0:1, :] + summed[1:2, :]
        hl_s[lane, 1:2, :] = summed[2:3, :] + summed[3:4, :]
        if first:
            for c in stores(lane):
                c.start()
        return carry

    lax.fori_loop(0, GROUP, lane_body, 0, unroll=True)
    rs_ref[...] = lane_join(s, rs_s)
    us_ref[...] = lane_join(s, us_s)
    hl_ref[...] = lane_join(s, hl_s)
    for lane in range(GROUP if first else 0):
        for c in stores(lane):
            c.wait()


def late_kernel(s, y_in, gx_in, y_ref, dv_ref, wx_ref, y_hbm, gx_hbm, gxt_ref, gx_s, dbuf, sems):
    rows = s.rows
    store_y = pltpu.make_async_copy(y_ref, y_hbm.at[:, s.span], sems.at[0])
    store_y.start()
    for c in range(s.width // LANES):
        at = slice(c * LANES, (c + 1) * LANES)
        wide = slice(s.base + c * LANES, s.base + (c + 1) * LANES)
        own = rows_own(dbuf.at[c % s.chunks], dv_ref[:, at], wx_ref[:, wide])
        gx_s[:, at] = own.astype(BF16)
        gxt_ref[:, at] = own[rows - HALO :, :]
    store_gx = pltpu.make_async_copy(gx_s, gx_hbm.at[:, s.span], sems.at[1])
    store_gx.start()
    store_y.wait()
    store_gx.wait()


def tail_kernel(parts, bc_ref, halo_ref, dtt_ref, al_ref, wbc_ref, bbc_ref, dbc_ref, dbc_other, *rest):
    n = len(parts)
    groups, rest = [rest[i * 7 : (i + 1) * 7] for i in range(n)], rest[7 * n :]
    gdt_ref, pk_ref, back_ref, gbc_ref, bbuf, dbuf = rest
    taps, rows = wbc_ref.shape[0], bc_ref.shape[0]
    join = lambda i: jnp.concatenate([g[i][...] for g in groups], axis=1)
    rate, cum = decay(dtt_ref[...], al_ref[...])
    inter = jnp.transpose(join(3))
    through = jnp.transpose(join(1)) + inter
    d_cum = jnp.transpose(join(0) + join(2)) - through
    link = join(4)
    heads = rate.shape[0]
    sums = jnp.transpose(link)
    d_last = jnp.sum(inter, axis=1, keepdims=True) + jnp.exp(cum[:, rows - 1 : rows]) * sums[:, 0:1]
    d_cum = d_cum + jnp.where(iota(d_cum.shape, 1) == rows - 1, d_last, 0.0)
    d_rate = dot(d_cum, lower_ones(rows), precision=EXACT)
    step = dtt_ref[...]
    gdt_ref[...] = through / step - jnp.exp(column(al_ref[...])) * d_rate
    gal = jnp.broadcast_to(jnp.sum(rate * d_rate, axis=1, keepdims=True), (heads, LANES))
    gal = jnp.transpose(gal)[0:1, :]

    width = halo_ref.shape[1] - bc_ref.shape[1]
    v = conv_into(bbuf, halo_ref[:, width:], bc_ref[...], wbc_ref[...], bbc_ref[...])
    dv = (dbc_ref[...].astype(F32) + dbc_other[...].astype(F32)) * silu_slope(v)
    own, before = conv_back(dbuf, dv, wbc_ref[...])
    gbc_ref[...] = own
    bc_rows = conv_weight_rows(bbuf, dv, taps)
    pk_ref[...] = jnp.zeros(pk_ref.shape, pk_ref.dtype)
    for s, g in zip(parts, groups):
        pk_ref[0 : taps + 1, s.span] = g[5][0 : taps + 1, :].astype(BF16)
        back_ref[:, s.span] = g[6][...]
    back_ref[:, width:] = before.astype(BF16)
    row = taps + 1
    pk_ref[row : row + 1, 0:heads] = gal.astype(BF16)
    pk_ref[row : row + 1, LANES : LANES + heads] = link[1:2, :].astype(BF16)
    for k, r in enumerate(bc_rows):
        at = 2 * LANES + k * r.shape[1]
        pk_ref[row : row + 1, at : at + r.shape[1]] = r.astype(BF16)


def rows_kernel(parts, gx_in, back_ref, gbc_ref, *rest):
    n = len(parts)
    tails, (gx_hbm, grad_bc, gxt, sem) = rest[:n], rest[n:]
    rows, width = gbc_ref.shape[0], gxt.shape[1]
    for s, t in zip(parts, tails):
        gxt[:, s.span] = (t[...] + back_ref[:, s.span].astype(F32)).astype(BF16)
    store = pltpu.make_async_copy(gxt, gx_hbm.at[rows - HALO : rows, :], sem)
    store.start()
    grad_bc[...] = gbc_ref[...].astype(BF16)
    tail = gbc_ref[rows - HALO : rows, :] + back_ref[:, width:].astype(F32)
    grad_bc[rows - HALO : rows, :] = tail.astype(BF16)
    store.wait()


def finish_kernel(taps, heads, pk_ref, other_ref, gwx_ref, gwbc_ref, gbx_ref, gal_ref, gsk_ref, gbbc_ref):
    total = pk_ref[...].astype(F32) + other_ref[...].astype(F32)
    gwx_ref[...] = total[0:taps, :]
    bc_width = gbbc_ref.shape[0]
    row = total[taps + 1 : taps + 2, :]
    for k in range(taps):
        at = 2 * LANES + k * bc_width
        gwbc_ref[k : k + 1, :] = row[:, at : at + bc_width]
    gbx_ref[...] = total[taps]
    row = total[taps + 1]
    gal_ref[...] = row[0:heads]
    gsk_ref[...] = row[LANES : LANES + heads]
    at = 2 * LANES + taps * bc_width
    gbbc_ref[...] = row[at : at + bc_width]


VMEM = pl.BlockSpec(memory_space=pltpu.VMEM)
SMEM = pl.BlockSpec(memory_space=pltpu.SMEM)
ANY = pl.BlockSpec(memory_space=pl.ANY)
HBM = pl.BlockSpec(memory_space=pltpu.HBM)


def call(kernel, name, args, in_specs, outs, out_specs, scratch, flops=0, after=(), aliases=None):
    n, extra = len(args), len(after)

    def body(*refs):
        kernel(*refs[:n], *refs[n + extra :])

    moved = sum(a.size * a.dtype.itemsize for a in (*args, *outs))
    return pl.pallas_call(
        body,
        name=name,
        out_shape=tuple(outs),
        in_specs=list(in_specs) + [ANY] * extra,
        out_specs=tuple(out_specs),
        scratch_shapes=scratch,
        input_output_aliases=aliases or {},
        compiler_params=pltpu.CompilerParams(vmem_limit_bytes=12 << 20),
        cost_estimate=pl.CostEstimate(flops=flops, bytes_accessed=moved, transcendentals=0),
    )(*args, *after)


def shift(value, count, steps):
    pairs = [(i, i + steps) for i in range(count) if 0 <= i + steps < count]
    return lax.ppermute(value, "ctx", pairs)


def swap(value, count, mask):
    return lax.ppermute(value, "ctx", [(i, i ^ mask) for i in range(count)])


def group_scan(ahead, back, every, count):
    found = []
    for sign, value in ((1, ahead), (-1, back)):
        total = shift(every, count, sign * GROUP)
        value = shift(value, count, sign * GROUP).astype(F32)
        step = GROUP
        while step < count:
            value = value + total[0:1] * shift(value.astype(BF16), count, sign * step).astype(F32)
            total = total * shift(total, count, sign * step)
            step *= 2
        found.append(value.astype(BF16))
    return found


def local(n_ctx, x_in, bc_in, step_dt, a_log, d_skip, conv_wx, conv_bx, conv_wbc, conv_bbc, grad_out):
    rows, width = x_in.shape
    heads, state = step_dt.shape[1], bc_in.shape[1] // 2
    head_dim = width // heads
    taps = conv_wx.shape[0]
    n_chunks = width // (GROUP * LANES)
    cut = (n_chunks + 1) // 2
    parts = [Part(rows, state, head_dim, 0, cut), Part(rows, state, head_dim, cut * GROUP * LANES, n_chunks - cut)]
    pair = n_ctx == 2 * GROUP
    index = lax.axis_index("ctx")
    place = jnp.stack([index % GROUP, index // GROUP]).astype(jnp.int32)
    sds = jax.ShapeDtypeStruct
    vm = pltpu.VMEM

    halo = shift(jnp.concatenate([x_in[-HALO:], bc_in[-HALO:]], axis=1), n_ctx, 1)
    msg_rows = state + 8
    per_head = vm((GROUP, rows, LANES), F32)
    bc_shape = (rows, 2 * state)

    def factors():
        small = (step_dt.T, a_log, d_skip, conv_bx, conv_bbc, bc_in, conv_wx, conv_wbc)
        args = [pltpu.with_memory_space_constraint(v, pltpu.HBM) for v in (x_in, grad_out, *small)]
        outs = []
        for s in parts:
            outs += [sds((rows, s.width), BF16)] * 3
        n_out = len(outs)
        outs += [sds(v.shape if v.ndim > 1 else (1, v.shape[0]), v.dtype) for v in small]
        found = call(
            functools.partial(factors_kernel, parts, len(small)),
            "factors",
            args,
            [HBM] * len(args),
            outs,
            [VMEM] * len(outs),
            [per_head, pltpu.SemaphoreType.DMA((2 * len(parts) + len(small),))] + [vm(v.shape, v.dtype) for v in small if v.ndim == 1],
        )
        return found[:3], found[3:6], *found[n_out:]

    def states(s, first, fac, extra, after=()):
        x, _, ges = fac
        args = (place, x, ges, step_t, al, halo, wx, bx, *extra)
        wide = sds((rows, s.width), BF16)
        msgs = [sds((msg_rows, 2 * s.lane_width), BF16)] * GROUP
        return call(
            functools.partial(states_kernel, s, first),
            "states",
            args,
            [SMEM] + [VMEM] * (len(args) - 1),
            ([sds(bc_shape, BF16)] if first else []) + [wide] * 2 + msgs,
            [VMEM] * ((3 if first else 2) + GROUP),
            [vm((GROUP, msg_rows, 2 * s.lane_width), BF16), per_head, vm((s.chunks, rows + HALO, LANES), F32)]
            + ([vm((rows + HALO, 2 * state), F32)] if first else []),
            4 * rows * s.width * state,
            after,
        )

    def exchange(messages):
        return [messages[0]] + [swap(messages[d], n_ctx, d) for d in range(1, GROUP)]

    def intra(s, first, fac, mx, d_scores, after=()):
        x, g = fac[:2]
        args = (x, g, mx, mbc, halo, step_t, al, skip, wx, bx) + (() if first else (d_scores,))
        per_row = vm((GROUP, 16, rows), F32)
        return call(
            functools.partial(intra_kernel, s, first),
            "intra",
            args,
            [VMEM] * len(args),
            [sds((rows, s.width), BF16)] * 2
            + [sds((rows, s.width), F32)] * 3
            + [sds((rows, s.heads), F32)] * 2
            + [sds((rows, rows) if first else bc_shape, F32)],
            [VMEM] * 8,
            [per_head, per_head, per_head, per_row, per_row, per_head, per_head, vm((s.chunks, rows + HALO, LANES), F32), vm((GROUP, HALO, LANES), F32)],
            12 * rows * s.width * rows,
            after,
        )

    def sums(s, blocks, after=()):
        shape = (state, s.lane_width)
        outs = [sds(shape, BF16)] if pair else [sds(shape, BF16)] * 2 + [sds((8, s.lane_width), F32)]
        summed = call(
            functools.partial(group_sum_kernel, s, pair),
            "group_sum",
            (place, *blocks),
            [SMEM] + [VMEM] * GROUP,
            outs,
            [VMEM] * len(outs),
            [vm((GROUP, msg_rows, 2 * s.lane_width), BF16)],
            state * s.width,
            after,
        )
        return [swap(summed[0], n_ctx, GROUP)] if pair else group_scan(*summed, n_ctx)

    def scan(s, blocks, before, after=()):
        return call(
            functools.partial(group_scan_kernel, s, pair),
            "group_scan",
            (place, *blocks, *before),
            [SMEM] + [VMEM] * GROUP + [VMEM] * len(before),
            [sds((state, 2 * s.lane_width), BF16)] * GROUP,
            [VMEM] * GROUP,
            [vm((GROUP, msg_rows, 2 * s.lane_width), BF16), vm((GROUP, state, 2 * s.lane_width), BF16)],
            state * s.width,
            after,
        )

    def pair_grads(s, wxs, ges, dbc, held, dtype, after=()):
        return call(
            functools.partial(pair_grads_kernel, s),
            "pair_grads",
            (place, wxs, ges, dbc, *held),
            [SMEM] + [VMEM] * 3 + [VMEM] * GROUP,
            [sds(bc_shape, dtype)],
            [VMEM],
            [vm((GROUP, state, 2 * s.lane_width), BF16)],
            4 * rows * s.width * state,
            after,
        )[0]

    def outputs(s, first, fac, mx, wxs, inner, held, after=()):
        x, g, ges = fac[:3]
        args = (place, x, g, mx, wxs, ges, mbc, halo, wx, *inner[:5], *held)
        if first:
            big, specs = [sds((rows, width), BF16)] * 2 + [sds((HALO, s.width), F32)], [HBM, HBM, VMEM]
        else:
            big, specs = [sds((rows, s.width), BF16), sds((rows, s.width), F32)], [VMEM, VMEM]
        return call(
            functools.partial(outputs_kernel, s, first),
            "outputs",
            args,
            [SMEM] + [VMEM] * (len(args) - 1),
            big
            + [sds((HALO, s.width), BF16), sds((8, s.width), F32)]
            + [sds((rows, s.heads), F32)] * 2
            + [sds((8, s.heads), F32)],
            specs + [VMEM] * 5,
            [
                vm((GROUP, state, 2 * s.lane_width), BF16),
                vm((s.chunks, rows + HALO, LANES), F32),
                vm((s.chunks, rows + 2 * HALO, LANES), F32),
                per_head,
                per_head,
                vm((GROUP, 8, LANES), F32),
            ]
            + ([vm((rows, s.width), BF16)] * 2 + [pltpu.SemaphoreType.DMA((2, GROUP))] if first else []),
            4 * rows * s.width * state,
            after,
        )

    def late(s, y, gx, y_part, dv):
        return call(
            functools.partial(late_kernel, s),
            "late",
            (y, gx, y_part, dv, wx),
            [HBM, HBM] + [VMEM] * 3,
            [sds((rows, width), BF16)] * 2 + [sds((HALO, s.width), F32)],
            [HBM, HBM, VMEM],
            [vm((rows, s.width), BF16), vm((s.chunks, rows + HALO, LANES), F32), pltpu.SemaphoreType.DMA((2,))],
            aliases={0: 0, 1: 1},
        )

    a, b = parts
    fac_a, fac_b, step_t, al, skip, bx, bbc, bc, wx, wbc = factors()
    mbc, mx_a, wxs_a, *msgs = states(a, True, fac_a, (bc, wbc, bbc))
    blocks_a = exchange(msgs)
    mx_b, wxs_b, *msgs = states(b, False, fac_b, (mbc,))
    blocks_b = exchange(msgs)
    inner_a = intra(a, True, fac_a, mx_a, None, (msgs[0],))
    before_a = sums(a, blocks_a, (inner_a[-1],))
    before_b = sums(b, blocks_b)
    inner_b = intra(b, False, fac_b, mx_b, inner_a[-1])
    held_a = exchange(scan(a, blocks_a, before_a, (inner_b[-1],)))
    held_b = exchange(scan(b, blocks_b, before_b))
    dbc = pair_grads(a, wxs_a, fac_a[2], inner_b[-1], held_a, F32)
    y, gx, tail_a, *out_a = outputs(a, True, fac_a, mx_a, wxs_a, inner_a, held_a)
    dbc = pair_grads(b, wxs_b, fac_b[2], dbc, held_b, BF16, (out_a[-1],))
    n_head = lax.axis_size("head")
    if n_head == 2:
        other = lax.ppermute(dbc, "head", [(0, 1), (1, 0)])
    else:
        other = (lax.psum(dbc.astype(F32), "head") - dbc.astype(F32)).astype(BF16)
    y_b, dv_b, *out_b = outputs(b, False, fac_b, mx_b, wxs_b, inner_b, held_b)

    args = [bc, halo, step_t, al, wbc, bbc, dbc, other]
    for inner, out in ((inner_a, out_a), (inner_b, out_b)):
        args += [inner[5], inner[6], out[2], out[3], out[4], out[1], out[0]]
    gdt_t, packed, back, gbc = call(
        functools.partial(tail_kernel, parts),
        "tail",
        tuple(args),
        [VMEM] * len(args),
        [sds((heads, rows), F32), sds((8, width), BF16), sds((HALO, width + 2 * state), BF16), sds(bc_shape, F32)],
        [VMEM] * 4,
        [vm((rows + HALO, 2 * state), F32), vm((rows + 2 * HALO, 2 * state), F32)],
    )
    y, gx, tail_b = late(b, y, gx, y_b, dv_b)
    back = shift(back, n_ctx, -1)
    step = 1
    while 2 * step < n_ctx:
        packed = packed + swap(packed, n_ctx, step)
        step *= 2
    last = swap(packed, n_ctx, step)
    args = (gx, back, gbc, tail_a, tail_b)
    gx, grad_bc = call(
        functools.partial(rows_kernel, parts),
        "rows",
        args,
        [HBM] + [VMEM] * (len(args) - 1),
        [sds((rows, width), BF16), sds(bc_shape, BF16)],
        [HBM, VMEM],
        [vm((HALO, width), BF16), pltpu.SemaphoreType.DMA],
        aliases={0: 0},
    )
    gwx, gwbc, gbx, gal, gskip, gbbc = call(
        functools.partial(finish_kernel, taps, heads),
        "finish",
        (packed, last),
        [VMEM] * 2,
        [sds((taps, width), F32), sds((taps, 2 * state), F32)] + [sds((n,), F32) for n in (width, heads, heads, 2 * state)],
        [VMEM] * 6,
        [],
    )
    return y, gx, grad_bc, gdt_t.T, gal, gskip, gwx, gbx, gwbc, gbbc


def solution(mesh):
    rows, both = P(("groups", "ctx"), "head"), P(("groups", "head"))
    return jax.shard_map(
        functools.partial(local, mesh.shape["ctx"]),
        mesh=mesh,
        in_specs=(rows, P(("groups", "ctx"), None), rows, P("head"), P("head"), P(None, "head"), P("head"), P(), P(), rows),
        out_specs=(rows, rows, P(("groups", "ctx"), None), rows, both, both, P("groups", "head"), both, P("groups", None), P("groups")),
        check_vma=False,
    )
```

```python
import functools

import jax
import jax.numpy as jnp
from jax import lax
from jax.experimental import pallas as pl
from jax.experimental.pallas import tpu as pltpu
from jax.sharding import PartitionSpec as P

F32, BF16 = jnp.float32, jnp.bfloat16
EXACT = lax.Precision.HIGHEST
LANES = 128
HALO = 8
GROUP = 4


def dot(a, b, ca=1, cb=0, precision=None):
    dims = (((ca,), (cb,)), ((), ()))
    return lax.dot_general(a, b, dims, preferred_element_type=F32, precision=precision)


def iota(shape, dim):
    return lax.broadcasted_iota(jnp.int32, shape, dim)


def lower_ones(size):
    return (iota((size, size), 0) >= iota((size, size), 1)).astype(F32)


def upper_ones(size):
    return (iota((size, size), 0) <= iota((size, size), 1)).astype(F32)


def sigmoid(v):
    return 1.0 / (1.0 + jnp.exp(-v))


def cols(start):
    return pl.ds(pl.multiple_of(start, LANES), LANES)


class Part:
    def __init__(self, rows, state, head_dim, base, chunks):
        self.rows, self.state, self.head_dim, self.base, self.chunks = rows, state, head_dim, base, chunks
        self.lane_width = chunks * LANES
        self.width = GROUP * self.lane_width
        self.per_chunk = LANES // head_dim
        self.lane_heads = chunks * self.per_chunk
        self.heads = GROUP * self.lane_heads
        self.head0 = base // head_dim
        self.span = slice(base, base + self.width)
        self.head_span = slice(self.head0, self.head0 + self.heads)


def lane_slices(s, value, scratch):
    for lane in range(GROUP):
        at = s.head0 + lane * s.lane_heads
        scratch[lane, :, 0 : s.lane_heads] = value[:, at : at + s.lane_heads]


def lane_join(s, scratch):
    return jnp.concatenate([scratch[lane][:, 0 : s.lane_heads] for lane in range(GROUP)], axis=1)


def spread(s, value, chunk):
    rows = value.shape[0]
    lane = iota((rows, LANES), 1)
    out = None
    for i in range(s.per_chunk):
        h = chunk * s.per_chunk + i
        col = jnp.broadcast_to(value[:, h : h + 1], (rows, LANES))
        out = col if out is None else jnp.where(lane >= i * s.head_dim, col, out)
    return out


def head_sums(s, value, chunk):
    r, c = iota((LANES, LANES), 0), iota((LANES, LANES), 1)
    one = (c == chunk * s.per_chunk + r // s.head_dim).astype(F32).astype(BF16)
    hi = value.astype(BF16)
    lo = (value - hi.astype(F32)).astype(BF16)
    return dot(jnp.concatenate([hi, lo], axis=1), jnp.concatenate([one, one], axis=0))


def column(row):
    return jnp.transpose(jnp.broadcast_to(row, (8, row.shape[1])))[:, 0:1]


def decay(step_t, alog):
    rate = -step_t * jnp.exp(column(alog))
    return rate, dot(rate, upper_ones(step_t.shape[1]), precision=EXACT)


def decay_factors(step_t, alog):
    _, cum = decay(step_t, alog)
    rows = step_t.shape[1]
    last = cum[:, rows - 1 : rows]
    return jnp.transpose(jnp.exp(cum)), jnp.transpose(jnp.exp(last - cum) * step_t)


def conv_into(buf, halo, x, weight, bias):
    rows = x.shape[0]
    buf[0:HALO, :] = halo.astype(F32)
    buf[HALO : HALO + rows, :] = x.astype(F32)
    taps = weight.shape[0]
    total = jnp.broadcast_to(bias, x.shape)
    for k in range(taps):
        first = HALO - (taps - 1) + k
        total = total + weight[k : k + 1, :] * buf[first : first + rows, :]
    return total


def factors_kernel(parts, n_small, x_hbm, g_hbm, *refs):
    n = len(parts)
    given, refs = refs[:n_small], refs[n_small:]
    outs, refs = [refs[3 * i : 3 * i + 3] for i in range(n)], refs[3 * n :]
    taken, refs = refs[:n_small], refs[n_small:]
    ecum_s, sems, *flat = refs
    targets = [flat.pop(0) if len(ref.shape) == 1 else to for ref, to in zip(given, taken)]
    small = [pltpu.make_async_copy(ref, to, sems.at[2 * n + k]) for k, (ref, to) in enumerate(zip(given, targets))]
    for c in small:
        c.start()
    loads = []
    for i, (s, out) in enumerate(zip(parts, outs)):
        loads.append(
            [
                pltpu.make_async_copy(g_hbm.at[:, s.span], out[1], sems.at[2 * i]),
                pltpu.make_async_copy(x_hbm.at[:, s.span], out[0], sems.at[2 * i + 1]),
            ]
        )
        for c in loads[-1]:
            c.start()
    for c in small:
        c.wait()
    for ref, at, to in zip(given, targets, taken):
        if len(ref.shape) == 1:
            to[...] = at[...][None, :]
    grow, _ = decay_factors(taken[0][...], taken[1][...])
    for s, out, load in zip(parts, outs, loads):
        _, g_ref, ges_ref = out
        lane_slices(s, grow, ecum_s)

        load[0].wait()

        def scale_body(lane, carry):
            for c in range(s.chunks):
                at = cols(lane * s.lane_width + c * LANES)
                ges_ref[:, at] = (g_ref[:, at].astype(F32) * spread(s, ecum_s[lane], c)).astype(BF16)
            return carry

        lax.fori_loop(0, GROUP, scale_body, 0, unroll=True)
    for load in loads:
        load[1].wait()


def states_kernel(s, first, lane_ref, x_ref, ges_ref, dtt_ref, al_ref, halo_ref, wx_ref, bx_ref, *rest):
    if first:
        bc_ref, wbc_ref, bbc_ref, mbc_ref, *rest = rest
    else:
        mbc_ref, *rest = rest
    mx_ref, wxs_ref = rest[:2]
    outs = rest[2 : 2 + GROUP]
    msg, endw_s, xbuf, *bbuf = rest[2 + GROUP :]
    me = lane_ref[0]
    grow, shrink = decay_factors(dtt_ref[...], al_ref[...])
    lane_slices(s, shrink, endw_s)
    total8 = jnp.broadcast_to(grow[s.rows - 1 : s.rows, s.head_span], (8, s.heads))
    if first:
        width = halo_ref.shape[1] - bc_ref.shape[1]
        v = conv_into(bbuf[0], halo_ref[:, width:], bc_ref[...], wbc_ref[...], bbc_ref[...])
        mbc_ref[...] = (v * sigmoid(v)).astype(BF16)
    mixed_bc = mbc_ref[...].astype(F32)
    b_t = jnp.transpose(mixed_bc[:, : s.state]).astype(BF16)
    c_t = jnp.transpose(mixed_bc[:, s.state :]).astype(BF16)

    def lane_body(lane, carry):
        base = lane * s.lane_width
        for c in range(s.chunks):
            at = cols(base + c * LANES)
            wide = cols(s.base + base + c * LANES)
            v = conv_into(xbuf.at[c], halo_ref[:, wide], x_ref[:, at], wx_ref[:, wide], bx_ref[:, wide])
            mixed = (v * sigmoid(v)).astype(BF16)
            mx_ref[:, at] = mixed
            wxs_ref[:, at] = (mixed.astype(F32) * spread(s, endw_s[lane], c)).astype(BF16)
        whole = pl.ds(pl.multiple_of(base, LANES), s.lane_width)
        rows, after = slice(0, s.state), slice(s.state, s.state + 8)
        msg[lane, rows, : s.lane_width] = dot(b_t, wxs_ref[:, whole]).astype(BF16)
        msg[lane, rows, s.lane_width :] = dot(c_t, ges_ref[:, whole]).astype(BF16)
        shape = (s.heads, s.lane_width)
        pick = (iota(shape, 0) == lane * s.lane_heads + iota(shape, 1) // s.head_dim).astype(F32)
        total = dot(total8, pick, precision=EXACT)
        hi = total.astype(BF16).astype(F32)
        mid = (total - hi).astype(BF16).astype(F32)
        row = iota(total.shape, 0)
        split = jnp.where(row == 0, hi, jnp.where(row == 1, mid, jnp.where(row == 2, total - hi - mid, 0.0)))
        msg[lane, after, : s.lane_width] = split.astype(BF16)
        msg[lane, after, s.lane_width :] = split.astype(BF16)
        return carry

    lax.fori_loop(0, GROUP, lane_body, 0, unroll=True)
    for d in range(GROUP):
        outs[d][...] = msg[me ^ d]


def intra_kernel(s, first, x_ref, g_ref, mx_ref, mbc_ref, halo_ref, dtt_ref, al_ref, dsk_ref, wx_ref, bx_ref, *rest):
    if first:
        y_ref, dx_ref, slope_ref, grow_ref, shrink_ref, rs_ref, vs_ref, ds_ref, *rest = rest
    else:
        ds_in, y_ref, dx_ref, slope_ref, grow_ref, shrink_ref, rs_ref, vs_ref, dbc_ref, *rest = rest
    cum_s, ecum_s, endw_s, cumt_s, dtt_s, rs_s, vs_s, xbuf, skip_s = rest
    rows = s.rows
    _, cum_t = decay(dtt_ref[...], al_ref[...])
    lane_slices(s, jnp.transpose(cum_t), cum_s)
    grow, shrink = decay_factors(dtt_ref[...], al_ref[...])
    lane_slices(s, grow, ecum_s)
    lane_slices(s, shrink, endw_s)
    skips = jnp.broadcast_to(dsk_ref[...], (HALO, dsk_ref.shape[1]))
    lane_slices(s, skips, skip_s)
    for lane in range(GROUP):
        at = s.head0 + lane * s.lane_heads
        cumt_s[lane, 0 : s.lane_heads, :] = cum_t[at : at + s.lane_heads, :]
        dtt_s[lane, 0 : s.lane_heads, :] = dtt_ref[at : at + s.lane_heads, :]
    b, c_m = mbc_ref[:, : s.state], mbc_ref[:, s.state :]
    causal = iota((rows, rows), 0) >= iota((rows, rows), 1)
    scores = jnp.where(causal, dot(c_m, b, 1, 1), 0.0)
    lane_id = iota((rows, LANES), 1)
    masks = [((lane_id >= i * s.head_dim) & (lane_id < (i + 1) * s.head_dim)).astype(F32).astype(BF16) for i in range(s.per_chunk)]

    def lane_body(lane, d_scores):
        base = lane * s.lane_width
        row_acc = jnp.zeros((rows, LANES), F32)
        col_acc = jnp.zeros((rows, LANES), F32)
        cum_l = cum_s[lane]
        for c in range(s.chunks):
            at = cols(base + c * LANES)
            wide = cols(s.base + base + c * LANES)
            x, g = mx_ref[:, at], g_ref[:, at]
            x_st = jnp.concatenate([x * m for m in masks], axis=0)
            g_st = jnp.concatenate([g * m for m in masks], axis=0)
            d_mix = dot(g_st, x, 1, 1)
            mixes = []
            for i in range(s.per_chunk):
                h = c * s.per_chunk + i
                gap = jnp.broadcast_to(cum_l[:, h : h + 1], (rows, rows)) - cumt_s[lane, h : h + 1, :]
                e = jnp.exp(jnp.minimum(gap, 0.0)) * dtt_s[lane, h : h + 1, :]
                mixes.append((e * scores).astype(BF16))
                d_scores = d_scores + d_mix[i * rows : (i + 1) * rows, :] * e
            y = dot(jnp.concatenate(mixes, axis=1), x_st)
            dx = dot(jnp.concatenate(mixes, axis=0), g_st, 0, 0)
            xf, gf, skip = x.astype(F32), g.astype(F32), spread(s, skip_s[lane], c)[0:1, :]
            row_acc = row_acc + head_sums(s, gf * y, c)
            col_acc = col_acc + head_sums(s, xf * dx, c)
            y_ref[:, at] = (y + skip * xf).astype(BF16)
            dx_ref[:, at] = (dx + skip * gf).astype(BF16)
            grow_ref[:, at] = spread(s, ecum_s[lane], c)
            shrink_ref[:, at] = spread(s, endw_s[lane], c)
            v = conv_into(xbuf.at[c], halo_ref[:, wide], x_ref[:, at], wx_ref[:, wide], bx_ref[:, wide])
            slope_ref[:, at] = silu_slope(v)
        rs_s[lane] = row_acc
        vs_s[lane] = col_acc
        return d_scores

    start = jnp.zeros((rows, rows), F32) if first else ds_in[...]
    d_scores = lax.fori_loop(0, GROUP, lane_body, start, unroll=True)
    rs_ref[...] = lane_join(s, rs_s)
    vs_ref[...] = lane_join(s, vs_s)
    if first:
        ds_ref[...] = d_scores
    else:
        d_scores = jnp.where(causal, d_scores, 0.0).astype(BF16)
        dbc_ref[:, : s.state] = dot(d_scores, c_m, 0, 0)
        dbc_ref[:, s.state :] = dot(d_scores, b)


def place_blocks(me, srcs, buf):
    for d in range(GROUP):
        buf[me ^ d] = srcs[d][...]


def total_row(s, buf, i, at):
    return jnp.sum(buf[i, s.state : s.state + 8, at].astype(F32), axis=0, keepdims=True)


def group_sum_kernel(s, pair, at_ref, *refs):
    srcs, buf = refs[:GROUP], refs[-1]
    outs = refs[GROUP:-1]
    me, high = at_ref[0], at_ref[1]
    place_blocks(me, srcs, buf)
    for c in range(s.chunks):
        at = slice(c * LANES, (c + 1) * LANES)
        at_r = slice(s.lane_width + c * LANES, s.lane_width + (c + 1) * LANES)
        totals = [total_row(s, buf, i, at) for i in range(GROUP)]
        ahead = jnp.zeros((s.state, LANES), F32)
        back = jnp.zeros((s.state, LANES), F32)
        every = jnp.ones((1, LANES), F32)
        for i in range(GROUP):
            ahead = totals[i] * ahead + buf[i, 0 : s.state, at].astype(F32)
            r = GROUP - 1 - i
            back = totals[r] * back + buf[r, 0 : s.state, at_r].astype(F32)
            every = every * totals[i]
        if pair:
            outs[0][:, at] = jnp.where(high == 0, ahead, back).astype(BF16)
        else:
            outs[0][:, at] = ahead.astype(BF16)
            outs[1][:, at] = back.astype(BF16)
            outs[2][:, at] = jnp.broadcast_to(every, (8, LANES))


def group_scan_kernel(s, pair, at_ref, *refs):
    srcs = refs[:GROUP]
    n_in = 1 if pair else 2
    before = refs[GROUP : GROUP + n_in]
    outs = refs[GROUP + n_in : 2 * GROUP + n_in]
    buf, done = refs[2 * GROUP + n_in :]
    me, high = at_ref[0], at_ref[1]
    place_blocks(me, srcs, buf)
    for c in range(s.chunks):
        at = slice(c * LANES, (c + 1) * LANES)
        at_r = slice(s.lane_width + c * LANES, s.lane_width + (c + 1) * LANES)
        totals = [total_row(s, buf, i, at) for i in range(GROUP)]
        first = before[0][:, at].astype(F32)
        if pair:
            ahead = jnp.where(high == 1, first, 0.0)
            back = jnp.where(high == 0, first, 0.0)
        else:
            ahead, back = first, before[1][:, at].astype(F32)
        for i in range(GROUP):
            done[i, :, at] = ahead.astype(BF16)
            r = GROUP - 1 - i
            done[r, :, at_r] = back.astype(BF16)
            if i < GROUP - 1:
                ahead = totals[i] * ahead + buf[i, 0 : s.state, at].astype(F32)
                back = totals[r] * back + buf[r, 0 : s.state, at_r].astype(F32)
    for d in range(GROUP):
        outs[d][...] = done[me ^ d]


def conv_back(buf, dv, weight):
    rows, taps = dv.shape[0], weight.shape[0]
    zeros = jnp.zeros((HALO, dv.shape[1]), F32)
    buf[0:HALO, :] = zeros
    buf[HALO : HALO + rows, :] = dv
    buf[HALO + rows : 2 * HALO + rows, :] = zeros
    own = before = None
    for k in range(taps):
        w = weight[k : k + 1, :]
        first = HALO + taps - 1 - k
        part = w * buf[first : first + rows, :]
        own = part if own is None else own + part
        first = taps - 1 - k
        part = w * buf[first : first + HALO, :]
        before = part if before is None else before + part
    keep = iota(before.shape, 0) >= HALO - (taps - 1)
    return own, jnp.where(keep, before, 0.0)


def rows_before(buf, dv, weight):
    taps = weight.shape[0]
    buf[0:HALO, :] = jnp.zeros((HALO, dv.shape[1]), F32)
    buf[HALO : 2 * HALO, :] = dv[0:HALO, :]
    before = None
    for k in range(taps):
        first = taps - 1 - k
        part = weight[k : k + 1, :] * buf[first : first + HALO, :]
        before = part if before is None else before + part
    return jnp.where(iota(before.shape, 0) >= HALO - (taps - 1), before, 0.0)


def rows_own(buf, dv, weight):
    rows, taps = dv.shape[0], weight.shape[0]
    buf[0:rows, :] = dv
    buf[rows : rows + HALO, :] = jnp.zeros((HALO, dv.shape[1]), F32)
    own = None
    for k in range(taps):
        first = taps - 1 - k
        part = weight[k : k + 1, :] * buf[first : first + rows, :]
        own = part if own is None else own + part
    return own


def conv_weight_rows(buf, dv, taps):
    rows = dv.shape[0]
    out = []
    for k in range(taps):
        first = HALO - (taps - 1) + k
        out.append(jnp.sum(dv * buf[first : first + rows, :], axis=0, keepdims=True))
    out.append(jnp.sum(dv, axis=0, keepdims=True))
    return out


def silu_slope(v):
    sig = sigmoid(v)
    return sig * (1.0 + v * (1.0 - sig))


def pair_grads_kernel(s, lane_ref, wxs_ref, ges_ref, dbc_in, *rest):
    srcs, (dbc_ref, held) = rest[:GROUP], rest[GROUP:]
    place_blocks(lane_ref[0], srcs, held)
    d_b, d_c = dbc_in[:, : s.state], dbc_in[:, s.state :]
    for lane in range(GROUP):
        whole = slice(lane * s.lane_width, (lane + 1) * s.lane_width)
        d_c = d_c + dot(ges_ref[:, whole], held[lane, :, : s.lane_width], 1, 1)
        d_b = d_b + dot(wxs_ref[:, whole], held[lane, :, s.lane_width :], 1, 1)
    dbc_ref[:, : s.state] = d_b.astype(dbc_ref.dtype)
    dbc_ref[:, s.state :] = d_c.astype(dbc_ref.dtype)


def outputs_kernel(s, first, lane_ref, x_ref, g_ref, mx_ref, wxs_ref, ges_ref, mbc_ref, halo_ref, wx_ref, yl_ref, dxl_ref, slope_ref, grow_ref, shrink_ref, *rest):
    srcs, rest = rest[:GROUP], rest[GROUP:]
    if first:
        y_hbm, gx_hbm, gxt_ref, *rest = rest
    else:
        y_s, dv_ref, *rest = rest
    ho_ref, pk_ref, rs_ref, us_ref, hl_ref, *rest = rest
    held, xbuf, dbuf, rs_s, us_s, hl_s, *rest = rest
    if first:
        y_s, gx_s, out_sems = rest
    place_blocks(lane_ref[0], srcs, held)

    def stores(lane):
        at = lane * s.lane_width
        here = pl.ds(pl.multiple_of(at, LANES), s.lane_width)
        there = pl.ds(pl.multiple_of(s.base + at, LANES), s.lane_width)
        return (
            pltpu.make_async_copy(y_s.at[:, here], y_hbm.at[:, there], out_sems.at[0, lane]),
            pltpu.make_async_copy(gx_s.at[:, here], gx_hbm.at[:, there], out_sems.at[1, lane]),
        )

    rows, taps = s.rows, wx_ref.shape[0]
    b, c_m = mbc_ref[:, : s.state], mbc_ref[:, s.state :]
    shape = (s.lane_width, LANES)
    pick = (iota(shape, 0) // s.head_dim == iota(shape, 1)).astype(F32).astype(BF16)
    hl_s[...] = jnp.zeros(hl_s.shape, F32)

    def lane_body(lane, carry):
        base = lane * s.lane_width
        row_acc = jnp.zeros((rows, LANES), F32)
        col_acc = jnp.zeros((rows, LANES), F32)
        links = []
        for c in range(s.chunks):
            at = cols(base + c * LANES)
            wide = cols(s.base + base + c * LANES)
            state = held[lane, :, c * LANES : (c + 1) * LANES]
            later = held[lane, :, s.lane_width + c * LANES : s.lane_width + (c + 1) * LANES]
            y = dot(c_m, state)
            row_acc = row_acc + head_sums(s, ges_ref[:, at].astype(F32) * y, c)
            y_s[:, at] = (yl_ref[:, at].astype(F32) + y * grow_ref[:, at]).astype(BF16)
            dx = dot(b, later)
            col_acc = col_acc + head_sums(s, wxs_ref[:, at].astype(F32) * dx, c)
            links.append(jnp.sum(state.astype(F32) * later.astype(F32), axis=0, keepdims=True))
            weight = wx_ref[:, wide]
            dv = (dxl_ref[:, at].astype(F32) + dx * shrink_ref[:, at]) * slope_ref[:, at]
            if first:
                own, before = conv_back(dbuf.at[c], dv, weight)
                gx_s[:, at] = own.astype(BF16)
                gxt_ref[:, at] = own[rows - HALO :, :]
            else:
                before = rows_before(dbuf.at[c], dv, weight)
                dv_ref[:, at] = dv
            ho_ref[:, at] = before.astype(BF16)
            buf = xbuf.at[c]
            buf[0:HALO, :] = halo_ref[:, wide].astype(F32)
            buf[HALO : HALO + rows, :] = x_ref[:, at].astype(F32)
            packed = conv_weight_rows(buf, dv, taps)
            packed.append(jnp.sum(g_ref[:, at].astype(F32) * mx_ref[:, at].astype(F32), axis=0, keepdims=True))
            packed.append(jnp.zeros((8 - len(packed), LANES), F32))
            pk_ref[:, at] = jnp.concatenate(packed, axis=0)
        rs_s[lane] = row_acc
        us_s[lane] = col_acc
        whole = pl.ds(pl.multiple_of(base, LANES), s.lane_width)
        skip = jnp.broadcast_to(pk_ref[taps + 1 : taps + 2, whole], (8, s.lane_width))
        link = jnp.broadcast_to(jnp.concatenate(links, axis=1), skip.shape)
        row = iota(skip.shape, 0)
        both = jnp.where(row < 2, link, skip)
        hi = both.astype(BF16).astype(F32)
        summed = dot(jnp.where(row % 2 == 0, hi, both - hi).astype(BF16), pick)
        hl_s[lane, 0:1, :] = summed[0:1, :] + summed[1:2, :]
        hl_s[lane, 1:2, :] = summed[2:3, :] + summed[3:4, :]
        if first:
            for c in stores(lane):
                c.start()
        return carry

    lax.fori_loop(0, GROUP, lane_body, 0, unroll=True)
    rs_ref[...] = lane_join(s, rs_s)
    us_ref[...] = lane_join(s, us_s)
    hl_ref[...] = lane_join(s, hl_s)
    for lane in range(GROUP if first else 0):
        for c in stores(lane):
            c.wait()


def late_kernel(s, y_in, gx_in, y_ref, dv_ref, wx_ref, y_hbm, gx_hbm, gxt_ref, gx_s, dbuf, sems):
    rows = s.rows
    store_y = pltpu.make_async_copy(y_ref, y_hbm.at[:, s.span], sems.at[0])
    store_y.start()
    for c in range(s.width // LANES):
        at = slice(c * LANES, (c + 1) * LANES)
        wide = slice(s.base + c * LANES, s.base + (c + 1) * LANES)
        own = rows_own(dbuf.at[c % s.chunks], dv_ref[:, at], wx_ref[:, wide])
        gx_s[:, at] = own.astype(BF16)
        gxt_ref[:, at] = own[rows - HALO :, :]
    store_gx = pltpu.make_async_copy(gx_s, gx_hbm.at[:, s.span], sems.at[1])
    store_gx.start()
    store_y.wait()
    store_gx.wait()


def tail_kernel(parts, bc_ref, halo_ref, dtt_ref, al_ref, wbc_ref, bbc_ref, dbc_ref, dbc_other, *rest):
    n = len(parts)
    groups, rest = [rest[i * 7 : (i + 1) * 7] for i in range(n)], rest[7 * n :]
    gdt_ref, pk_ref, back_ref, gbc_ref, bbuf, dbuf = rest
    taps, rows = wbc_ref.shape[0], bc_ref.shape[0]
    rate, cum = decay(dtt_ref[...], al_ref[...])
    turned = lambda value: jnp.concatenate([jnp.transpose(value(g)) for g in groups], axis=0)
    inter = turned(lambda g: g[3][...])
    through = turned(lambda g: g[1][...]) + inter
    d_cum = turned(lambda g: g[0][...] + g[2][...]) - through
    link = jnp.concatenate([g[4][...] for g in groups], axis=1)
    heads = rate.shape[0]
    sums = turned(lambda g: g[4][...])
    d_last = jnp.sum(inter, axis=1, keepdims=True) + jnp.exp(cum[:, rows - 1 : rows]) * sums[:, 0:1]
    d_cum = d_cum + jnp.where(iota(d_cum.shape, 1) == rows - 1, d_last, 0.0)
    d_rate = dot(d_cum, lower_ones(rows), precision=EXACT)
    step = dtt_ref[...]
    gdt_ref[...] = through / step - jnp.exp(column(al_ref[...])) * d_rate
    gal = jnp.broadcast_to(jnp.sum(rate * d_rate, axis=1, keepdims=True), (heads, LANES))
    gal = jnp.transpose(gal)[0:1, :]

    width = halo_ref.shape[1] - bc_ref.shape[1]
    v = conv_into(bbuf, halo_ref[:, width:], bc_ref[...], wbc_ref[...], bbc_ref[...])
    dv = (dbc_ref[...].astype(F32) + dbc_other[...].astype(F32)) * silu_slope(v)
    own, before = conv_back(dbuf, dv, wbc_ref[...])
    gbc_ref[...] = own
    bc_rows = conv_weight_rows(bbuf, dv, taps)
    pk_ref[...] = jnp.zeros(pk_ref.shape, pk_ref.dtype)
    for s, g in zip(parts, groups):
        pk_ref[0 : taps + 1, s.span] = g[5][0 : taps + 1, :].astype(BF16)
        back_ref[:, s.span] = g[6][...]
    back_ref[:, width:] = before.astype(BF16)
    row = taps + 1
    pk_ref[row : row + 1, 0:heads] = gal.astype(BF16)
    pk_ref[row : row + 1, LANES : LANES + heads] = link[1:2, :].astype(BF16)
    for k, r in enumerate(bc_rows):
        at = 2 * LANES + k * r.shape[1]
        pk_ref[row : row + 1, at : at + r.shape[1]] = r.astype(BF16)


def rows_kernel(parts, gx_in, back_ref, gbc_ref, *rest):
    n = len(parts)
    tails, (gx_hbm, grad_bc, gxt, sem) = rest[:n], rest[n:]
    rows, width = gbc_ref.shape[0], gxt.shape[1]
    for s, t in zip(parts, tails):
        gxt[:, s.span] = (t[...] + back_ref[:, s.span].astype(F32)).astype(BF16)
    store = pltpu.make_async_copy(gxt, gx_hbm.at[rows - HALO : rows, :], sem)
    store.start()
    grad_bc[...] = gbc_ref[...].astype(BF16)
    tail = gbc_ref[rows - HALO : rows, :] + back_ref[:, width:].astype(F32)
    grad_bc[rows - HALO : rows, :] = tail.astype(BF16)
    store.wait()


def finish_kernel(taps, heads, pk_ref, other_ref, gwx_ref, gwbc_ref, gbx_ref, gal_ref, gsk_ref, gbbc_ref):
    total = pk_ref[...].astype(F32) + other_ref[...].astype(F32)
    gwx_ref[...] = total[0:taps, :]
    bc_width = gbbc_ref.shape[0]
    row = total[taps + 1 : taps + 2, :]
    for k in range(taps):
        at = 2 * LANES + k * bc_width
        gwbc_ref[k : k + 1, :] = row[:, at : at + bc_width]
    gbx_ref[...] = total[taps]
    row = total[taps + 1]
    gal_ref[...] = row[0:heads]
    gsk_ref[...] = row[LANES : LANES + heads]
    at = 2 * LANES + taps * bc_width
    gbbc_ref[...] = row[at : at + bc_width]


VMEM = pl.BlockSpec(memory_space=pltpu.VMEM)
SMEM = pl.BlockSpec(memory_space=pltpu.SMEM)
ANY = pl.BlockSpec(memory_space=pl.ANY)
HBM = pl.BlockSpec(memory_space=pltpu.HBM)


def call(kernel, name, args, in_specs, outs, out_specs, scratch, flops=0, after=(), aliases=None):
    n, extra = len(args), len(after)

    def body(*refs):
        kernel(*refs[:n], *refs[n + extra :])

    moved = sum(a.size * a.dtype.itemsize for a in (*args, *outs))
    return pl.pallas_call(
        body,
        name=name,
        out_shape=tuple(outs),
        in_specs=list(in_specs) + [ANY] * extra,
        out_specs=tuple(out_specs),
        scratch_shapes=scratch,
        input_output_aliases=aliases or {},
        compiler_params=pltpu.CompilerParams(vmem_limit_bytes=12 << 20),
        cost_estimate=pl.CostEstimate(flops=flops, bytes_accessed=moved, transcendentals=0),
    )(*args, *after)


def shift(value, count, steps):
    pairs = [(i, i + steps) for i in range(count) if 0 <= i + steps < count]
    return lax.ppermute(value, "ctx", pairs)


def swap(value, count, mask):
    return lax.ppermute(value, "ctx", [(i, i ^ mask) for i in range(count)])


def group_scan(ahead, back, every, count):
    found = []
    for sign, value in ((1, ahead), (-1, back)):
        total = shift(every, count, sign * GROUP)
        value = shift(value, count, sign * GROUP).astype(F32)
        step = GROUP
        while step < count:
            value = value + total[0:1] * shift(value.astype(BF16), count, sign * step).astype(F32)
            total = total * shift(total, count, sign * step)
            step *= 2
        found.append(value.astype(BF16))
    return found


def local(n_ctx, x_in, bc_in, step_dt, a_log, d_skip, conv_wx, conv_bx, conv_wbc, conv_bbc, grad_out):
    rows, width = x_in.shape
    heads, state = step_dt.shape[1], bc_in.shape[1] // 2
    head_dim = width // heads
    taps = conv_wx.shape[0]
    n_chunks = width // (GROUP * LANES)
    cut = (n_chunks + 1) // 2
    parts = [Part(rows, state, head_dim, 0, cut), Part(rows, state, head_dim, cut * GROUP * LANES, n_chunks - cut)]
    pair = n_ctx == 2 * GROUP
    index = lax.axis_index("ctx")
    place = jnp.stack([index % GROUP, index // GROUP]).astype(jnp.int32)
    sds = jax.ShapeDtypeStruct
    vm = pltpu.VMEM

    halo = shift(jnp.concatenate([x_in[-HALO:], bc_in[-HALO:]], axis=1), n_ctx, 1)
    msg_rows = state + 8
    per_head = vm((GROUP, rows, LANES), F32)
    bc_shape = (rows, 2 * state)

    def factors():
        small = (step_dt.T, a_log, d_skip, conv_bx, conv_bbc, bc_in, conv_wx, conv_wbc)
        args = [pltpu.with_memory_space_constraint(v, pltpu.HBM) for v in (x_in, grad_out, *small)]
        outs = []
        for s in parts:
            outs += [sds((rows, s.width), BF16)] * 3
        n_out = len(outs)
        outs += [sds(v.shape if v.ndim > 1 else (1, v.shape[0]), v.dtype) for v in small]
        found = call(
            functools.partial(factors_kernel, parts, len(small)),
            "factors",
            args,
            [HBM] * len(args),
            outs,
            [VMEM] * len(outs),
            [per_head, pltpu.SemaphoreType.DMA((2 * len(parts) + len(small),))] + [vm(v.shape, v.dtype) for v in small if v.ndim == 1],
        )
        return found[:3], found[3:6], *found[n_out:]

    def states(s, first, fac, extra, after=()):
        x, _, ges = fac
        args = (place, x, ges, step_t, al, halo, wx, bx, *extra)
        wide = sds((rows, s.width), BF16)
        msgs = [sds((msg_rows, 2 * s.lane_width), BF16)] * GROUP
        return call(
            functools.partial(states_kernel, s, first),
            "states",
            args,
            [SMEM] + [VMEM] * (len(args) - 1),
            ([sds(bc_shape, BF16)] if first else []) + [wide] * 2 + msgs,
            [VMEM] * ((3 if first else 2) + GROUP),
            [vm((GROUP, msg_rows, 2 * s.lane_width), BF16), per_head, vm((s.chunks, rows + HALO, LANES), F32)]
            + ([vm((rows + HALO, 2 * state), F32)] if first else []),
            4 * rows * s.width * state,
            after,
        )

    def exchange(messages):
        return [messages[0]] + [swap(messages[d], n_ctx, d) for d in range(1, GROUP)]

    def intra(s, first, fac, mx, d_scores, after=()):
        x, g = fac[:2]
        args = (x, g, mx, mbc, halo, step_t, al, skip, wx, bx) + (() if first else (d_scores,))
        per_row = vm((GROUP, 16, rows), F32)
        return call(
            functools.partial(intra_kernel, s, first),
            "intra",
            args,
            [VMEM] * len(args),
            [sds((rows, s.width), BF16)] * 2
            + [sds((rows, s.width), F32)] * 3
            + [sds((rows, s.heads), F32)] * 2
            + [sds((rows, rows) if first else bc_shape, F32)],
            [VMEM] * 8,
            [per_head, per_head, per_head, per_row, per_row, per_head, per_head, vm((s.chunks, rows + HALO, LANES), F32), vm((GROUP, HALO, LANES), F32)],
            12 * rows * s.width * rows,
            after,
        )

    def sums(s, blocks, after=()):
        shape = (state, s.lane_width)
        outs = [sds(shape, BF16)] if pair else [sds(shape, BF16)] * 2 + [sds((8, s.lane_width), F32)]
        summed = call(
            functools.partial(group_sum_kernel, s, pair),
            "group_sum",
            (place, *blocks),
            [SMEM] + [VMEM] * GROUP,
            outs,
            [VMEM] * len(outs),
            [vm((GROUP, msg_rows, 2 * s.lane_width), BF16)],
            state * s.width,
            after,
        )
        return [swap(summed[0], n_ctx, GROUP)] if pair else group_scan(*summed, n_ctx)

    def scan(s, blocks, before, after=()):
        return call(
            functools.partial(group_scan_kernel, s, pair),
            "group_scan",
            (place, *blocks, *before),
            [SMEM] + [VMEM] * GROUP + [VMEM] * len(before),
            [sds((state, 2 * s.lane_width), BF16)] * GROUP,
            [VMEM] * GROUP,
            [vm((GROUP, msg_rows, 2 * s.lane_width), BF16), vm((GROUP, state, 2 * s.lane_width), BF16)],
            state * s.width,
            after,
        )

    def pair_grads(s, wxs, ges, dbc, held, dtype, after=()):
        return call(
            functools.partial(pair_grads_kernel, s),
            "pair_grads",
            (place, wxs, ges, dbc, *held),
            [SMEM] + [VMEM] * 3 + [VMEM] * GROUP,
            [sds(bc_shape, dtype)],
            [VMEM],
            [vm((GROUP, state, 2 * s.lane_width), BF16)],
            4 * rows * s.width * state,
            after,
        )[0]

    def outputs(s, first, fac, mx, wxs, inner, held, after=()):
        x, g, ges = fac[:3]
        args = (place, x, g, mx, wxs, ges, mbc, halo, wx, *inner[:5], *held)
        if first:
            big, specs = [sds((rows, width), BF16)] * 2 + [sds((HALO, s.width), F32)], [HBM, HBM, VMEM]
        else:
            big, specs = [sds((rows, s.width), BF16), sds((rows, s.width), F32)], [VMEM, VMEM]
        return call(
            functools.partial(outputs_kernel, s, first),
            "outputs",
            args,
            [SMEM] + [VMEM] * (len(args) - 1),
            big
            + [sds((HALO, s.width), BF16), sds((8, s.width), F32)]
            + [sds((rows, s.heads), F32)] * 2
            + [sds((8, s.heads), F32)],
            specs + [VMEM] * 5,
            [
                vm((GROUP, state, 2 * s.lane_width), BF16),
                vm((s.chunks, rows + HALO, LANES), F32),
                vm((s.chunks, rows + 2 * HALO, LANES), F32),
                per_head,
                per_head,
                vm((GROUP, 8, LANES), F32),
            ]
            + ([vm((rows, s.width), BF16)] * 2 + [pltpu.SemaphoreType.DMA((2, GROUP))] if first else []),
            4 * rows * s.width * state,
            after,
        )

    def late(s, y, gx, y_part, dv):
        return call(
            functools.partial(late_kernel, s),
            "late",
            (y, gx, y_part, dv, wx),
            [HBM, HBM] + [VMEM] * 3,
            [sds((rows, width), BF16)] * 2 + [sds((HALO, s.width), F32)],
            [HBM, HBM, VMEM],
            [vm((rows, s.width), BF16), vm((s.chunks, rows + HALO, LANES), F32), pltpu.SemaphoreType.DMA((2,))],
            aliases={0: 0, 1: 1},
        )

    a, b = parts
    fac_a, fac_b, step_t, al, skip, bx, bbc, bc, wx, wbc = factors()
    mbc, mx_a, wxs_a, *msgs = states(a, True, fac_a, (bc, wbc, bbc))
    blocks_a = exchange(msgs)
    mx_b, wxs_b, *msgs = states(b, False, fac_b, (mbc,))
    blocks_b = exchange(msgs)
    inner_a = intra(a, True, fac_a, mx_a, None, (msgs[0],))
    before_a = sums(a, blocks_a, (inner_a[-1],))
    before_b = sums(b, blocks_b)
    inner_b = intra(b, False, fac_b, mx_b, inner_a[-1])
    held_a = exchange(scan(a, blocks_a, before_a, (inner_b[-1],)))
    held_b = exchange(scan(b, blocks_b, before_b))
    dbc = pair_grads(a, wxs_a, fac_a[2], inner_b[-1], held_a, F32)
    y, gx, tail_a, *out_a = outputs(a, True, fac_a, mx_a, wxs_a, inner_a, held_a)
    dbc = pair_grads(b, wxs_b, fac_b[2], dbc, held_b, BF16, (out_a[-1],))
    n_head = lax.axis_size("head")
    if n_head == 2:
        other = lax.ppermute(dbc, "head", [(0, 1), (1, 0)])
    else:
        other = (lax.psum(dbc.astype(F32), "head") - dbc.astype(F32)).astype(BF16)
    y_b, dv_b, *out_b = outputs(b, False, fac_b, mx_b, wxs_b, inner_b, held_b)

    args = [bc, halo, step_t, al, wbc, bbc, dbc, other]
    for inner, out in ((inner_a, out_a), (inner_b, out_b)):
        args += [inner[5], inner[6], out[2], out[3], out[4], out[1], out[0]]
    gdt_t, packed, back, gbc = call(
        functools.partial(tail_kernel, parts),
        "tail",
        tuple(args),
        [VMEM] * len(args),
        [sds((heads, rows), F32), sds((8, width), BF16), sds((HALO, width + 2 * state), BF16), sds(bc_shape, F32)],
        [VMEM] * 4,
        [vm((rows + HALO, 2 * state), F32), vm((rows + 2 * HALO, 2 * state), F32)],
    )
    y, gx, tail_b = late(b, y, gx, y_b, dv_b)
    back = shift(back, n_ctx, -1)
    step = 1
    while 2 * step < n_ctx:
        packed = packed + swap(packed, n_ctx, step)
        if step == 1:
            packed, tail_b = lax.optimization_barrier((packed, tail_b))
        step *= 2
    last = swap(packed, n_ctx, step)
    args = (gx, back, gbc, tail_a, tail_b)
    gx, grad_bc = call(
        functools.partial(rows_kernel, parts),
        "rows",
        args,
        [HBM] + [VMEM] * (len(args) - 1),
        [sds((rows, width), BF16), sds(bc_shape, BF16)],
        [HBM, VMEM],
        [vm((HALO, width), BF16), pltpu.SemaphoreType.DMA],
        aliases={0: 0},
    )
    gwx, gwbc, gbx, gal, gskip, gbbc = call(
        functools.partial(finish_kernel, taps, heads),
        "finish",
        (packed, last),
        [VMEM] * 2,
        [sds((taps, width), F32), sds((taps, 2 * state), F32)] + [sds((n,), F32) for n in (width, heads, heads, 2 * state)],
        [VMEM] * 6,
        [],
    )
    return y, gx, grad_bc, gdt_t.T, gal, gskip, gwx, gbx, gwbc, gbbc


def solution(mesh):
    rows, both = P(("groups", "ctx"), "head"), P(("groups", "head"))
    return jax.shard_map(
        functools.partial(local, mesh.shape["ctx"]),
        mesh=mesh,
        in_specs=(rows, P(("groups", "ctx"), None), rows, P("head"), P("head"), P(None, "head"), P("head"), P(), P(), rows),
        out_specs=(rows, rows, P(("groups", "ctx"), None), rows, both, both, P("groups", "head"), both, P("groups", None), P("groups")),
        check_vma=False,
    )
```
